32 devices in a mesh: dp: 8 (over y, x, core), tensor: 4 (over z).
Axes of the slice: x: 2, y: 2, z: 4, core: 2. Of those that a mesh axis runs over, the one named last changes fastest.
Arguments:
- queries: bfloat16 [256, 32, 16384], P('dp', None, 'tensor'), may hold values from -6 to 6
- key_rows: bfloat16 [256, 32, 1024], P(('dp', 'tensor')), may hold values from -6 to 6
- value_rows: bfloat16 [256, 32, 1024], P(('dp', 'tensor')), may hold values from -6 to 6
- destination: int32 [256], P('dp'), may hold values from 0 to 7, as said below
- token_count: int32 [256], P('dp'), may hold values from 16 to 32, as said below
- doc_ids: int32 [8, 1024], P('dp'), may hold values from 0 to 7, never falling along the last dimension, each value on 1 to 256 neighbouring positions
Outputs:
- attended: bfloat16 [8192, 16384], P('dp', 'tensor')
The draws below stay inside these ranges and needn't reach their ends.
Inputs may be any that keep to these rules, and one draw needn't show every extreme that they name: `destination`: every data group is named by exactly 32 sentences; of the 32 sentences of one group at most 8 name the same group, and some group sends exactly 8 sentences to one group in every draw. `token_count`: in every draw some data group receives only sentences with 32 live tokens, so its total is 1024.
All inputs are finite; a program needn't handle non-finite values.
Results may differ from the reference program's by a relative error of at most 0.0034.
Values may be sent and summed in bfloat16 or wider, within the bound.
A program may use at most 256 MiB of HBM per device.

```python
import math
import jax
import jax.numpy as jnp
import numpy as np
from jax import lax

HEADS = 128
KV_HEADS = 8
HEAD_DIM = 128
SENT = 32
SLOT = 32
ROW = 1024
CAP = 8
N_DP = 8


def draw_queries(key, part):
    shape = (N_DP * SENT, SLOT, HEADS, HEAD_DIM)
    base = jnp.clip(jax.random.normal(jax.random.fold_in(key, 34), shape, jnp.float32), -6.0, 6.0)
    return base.reshape(N_DP * SENT, SLOT, HEADS * HEAD_DIM).astype(jnp.bfloat16)


def draw_key_rows(key, part):
    shape = (N_DP * SENT, SLOT, KV_HEADS, HEAD_DIM)
    base = jnp.clip(jax.random.normal(jax.random.fold_in(key, 44), shape, jnp.float32), -6.0, 6.0)
    return base.reshape(N_DP * SENT, SLOT, KV_HEADS * HEAD_DIM).astype(jnp.bfloat16)


def draw_destination(key, part):
    sigma = jax.random.permutation(jax.random.fold_in(key, 11), N_DP)
    tau = jax.random.permutation(jax.random.fold_in(key, 12), N_DP)
    spare = jax.random.permutation(jax.random.fold_in(key, 13), jnp.arange(CAP * (N_DP - 1), dtype=jnp.int32) % (N_DP - 1)) + 1
    offsets = jnp.concatenate([jnp.zeros((CAP,), jnp.int32), spare[:SENT - CAP].astype(jnp.int32)])
    source_keys = jax.random.split(jax.random.fold_in(key, 14), N_DP)
    shuffles = jax.vmap(lambda one_key: jax.random.permutation(one_key, SENT))(source_keys)
    lanes = offsets[shuffles]
    target = sigma[(tau[:, None] + lanes) % N_DP]
    return target.reshape(N_DP * SENT).astype(jnp.int32)


def draw_token_count(key, part):
    levels = jax.random.randint(jax.random.fold_in(key, 21), (N_DP, 1), 2, 5)
    raw = jax.random.randint(jax.random.fold_in(key, 22), (N_DP, SENT), 0, SLOT // 2 + 1)
    counts = (SLOT // 2 + raw * levels // 4).reshape(N_DP * SENT)
    counts = jnp.minimum(counts, SLOT)
    routed = draw_destination(key, part)
    counts = jnp.where(routed == routed[0], SLOT, counts)
    return counts.astype(jnp.int32)


def block_scale(own_key, extent, cuts, smallest, largest):
    loudness, own = 1.0, jax.random.fold_in(own_key, 6)
    for dim, shards_of in cuts:
        heights = jnp.exp(jax.random.uniform(jax.random.fold_in(own, dim), (shards_of,), jnp.float32, smallest / len(cuts), largest / len(cuts)))
        loudness = loudness * jnp.repeat(heights, extent[dim] // shards_of).reshape([-1 if axis == dim else 1 for axis in range(len(extent))])
    return loudness


def profile(number_of, total, limit, skew):
    portions = [(1 << 20) // math.isqrt(standing ** skew) + 1 for standing in range(2, number_of + 1)]
    rest, given = total - limit - (number_of - 1), [1] * (number_of - 1)
    while rest > 0:
        candidates = [i for i in range(number_of - 1) if given[i] < limit]
        mass, budget = sum([portions[i] for i in candidates]), rest
        for i in candidates:
            extra = min(limit - given[i], max(1, budget * portions[i] // mass), rest)
            given[i] = given[i] + extra
            rest = rest - extra
    return np.array([limit] + given)


def ragged_sizes(rng, number_of, total, bound, skew):
    if number_of == 2:
        one = jax.random.randint(rng, (), max(1, total - bound), min(bound, total - 1) + 1)
        return jnp.stack([one, total - one])
    lengths = jnp.asarray(profile(number_of, total, bound, skew), jnp.int32)
    pairs = (number_of - 1) // 2
    source_of, sink = lengths[1:1 + 2 * pairs:2], lengths[2:2 + 2 * pairs:2]
    room = jnp.minimum(source_of - 1, bound - sink)
    moved = jax.random.randint(jax.random.fold_in(rng, 1), (pairs,), 0, 1 << 20) % (room + 1)
    lengths = lengths.at[1:1 + 2 * pairs:2].set(source_of - moved).at[2:2 + 2 * pairs:2].set(sink + moved)
    return lengths[jax.random.permutation(jax.random.fold_in(rng, 2), number_of)]


def centred(stream_key, dims, scale, bound, cuts=(), kind=jnp.bfloat16):
    values = scale * jax.random.normal(stream_key, dims, jnp.float32)
    if cuts:
        values = values * block_scale(stream_key, dims, cuts, -0.22, 0.18)
    return jnp.clip(values, -bound, bound).astype(kind)


def setup_inputs(seed: int = 0) -> dict:
    key_list = jax.random.split(jax.random.key(seed), 7)
    queries = draw_queries(jax.random.fold_in(key_list[6], 71), 0)
    key_rows = draw_key_rows(jax.random.fold_in(key_list[6], 71), 0)
    value_rows = centred(key_list[2], (N_DP * SENT, SLOT, KV_HEADS * HEAD_DIM), 1.0, 6.0, ((0, 32),))
    destination = draw_destination(jax.random.fold_in(key_list[6], 71), 0)
    token_count = draw_token_count(jax.random.fold_in(key_list[6], 71), 0)
    doc_ids = jax.vmap(lambda own: jnp.searchsorted(jnp.cumsum(ragged_sizes(own, 8, ROW, ROW // 4, 2)), jnp.arange(ROW), side="right"))(jax.random.split(key_list[5], N_DP)).reshape((N_DP, ROW)).astype(jnp.int32)
    return dict(queries=queries, key_rows=key_rows, value_rows=value_rows, destination=destination, token_count=token_count, doc_ids=doc_ids)


def pack_group(group, queries, key_rows, value_rows, destination, token_count):
    chosen = destination == group
    live = jnp.where(chosen, token_count, 0).astype(jnp.int32)
    ends = jnp.cumsum(live).astype(jnp.int32)
    starts = ends - live
    total = ends[-1]
    place = jnp.arange(ROW, dtype=jnp.int32)
    which = jnp.sum((place[:, None] >= ends[None, :]).astype(jnp.int32), axis=1).astype(jnp.int32)
    which = jnp.minimum(which, destination.shape[0] - 1)
    offset = jnp.clip(place - starts[which], 0, SLOT - 1).astype(jnp.int32)
    return queries[which, offset], key_rows[which, offset], value_rows[which, offset], total


def reference(queries, key_rows, value_rows, destination, token_count, doc_ids):
    group_size = HEADS // KV_HEADS
    scale_factor = HEAD_DIM ** -0.5

    def one_group(group):
        packed_q, packed_k, packed_v, total = pack_group(group, queries, key_rows, value_rows, destination, token_count)
        docs = lax.dynamic_index_in_dim(doc_ids, group, 0, keepdims=False)
        place = jnp.arange(ROW, dtype=jnp.int32)
        allowed = (place[None, :] <= place[:, None]) & (docs[None, :] == docs[:, None]) & (place[:, None] < total)
        q_heads = jnp.transpose(packed_q.reshape(ROW, HEADS, HEAD_DIM), (1, 0, 2))
        k_heads = jnp.transpose(packed_k.reshape(ROW, KV_HEADS, HEAD_DIM), (1, 0, 2))
        v_heads = jnp.transpose(packed_v.reshape(ROW, KV_HEADS, HEAD_DIM), (1, 0, 2))
        head_kv = (jnp.arange(HEADS, dtype=jnp.int32) // group_size).astype(jnp.int32)

        def one_head(item):
            q_head, kv_index = item
            k_head = lax.dynamic_index_in_dim(k_heads, kv_index, 0, keepdims=False)
            v_head = lax.dynamic_index_in_dim(v_heads, kv_index, 0, keepdims=False)
            scores = jnp.dot(q_head, k_head.T, preferred_element_type=jnp.float32) * scale_factor
            peak = jnp.max(jnp.where(allowed, scores, -1e30), axis=1, keepdims=True)
            weight = jnp.where(allowed, jnp.exp(scores - peak), 0.0)
            norm = jnp.sum(weight, axis=1, keepdims=True)
            mixed = jnp.dot(weight.astype(jnp.bfloat16), v_head, preferred_element_type=jnp.float32)
            return jnp.where(norm > 0, mixed / jnp.where(norm > 0, norm, 1.0), 0.0)

        outputs = lax.map(one_head, (q_heads, head_kv))
        return jnp.transpose(outputs, (1, 0, 2)).reshape(ROW, HEADS * HEAD_DIM).astype(jnp.bfloat16)

    result = lax.map(one_group, jnp.arange(N_DP, dtype=jnp.int32))
    return result.reshape(N_DP * ROW, HEADS * HEAD_DIM)
```

```python
import functools
import jax
import jax.numpy as jnp
from jax import lax
from jax.experimental import pallas as pl
from jax.experimental.pallas import tpu as pltpu
from jax.sharding import PartitionSpec as P

HEAD_DIM = 128
DOC_MAX = 256
LEAST = 16
TILE = 128
CHUNK_HEADS = 8
STACK = 4
SEND_TILE = 112
SPREAD = 12
SLOT = 32
SMALL = 1
UNROLLED = 8
VMEM = 56 << 20
ROUNDS = (256, 512, 512, 512, 256)
TIERS = (512, 560, 608, 704)
FAR = 1 << 20
CODE, START, COUNT, FIRST, INTO, TIER, PLAN = 0, 64, 128, 192, 256, 320, 336
NEG = -1e30
LOG2E = 1.4426950408889634
WHOLE = pl.BlockSpec(memory_space=pltpu.VMEM)
ANYWHERE = pl.BlockSpec(memory_space=pl.ANY)
FAR_OFF = pl.BlockSpec(memory_space=pltpu.HBM)
SCALARS = pl.BlockSpec(memory_space=pltpu.SMEM)


def fetch(code_ref, sources, cols, bases, buf, sem):
    def one(k, carry):
        code = code_ref[k]
        for i, (source, col) in enumerate(zip(sources, cols)):

            def start(i=i, source=source, col=col):
                pltpu.make_async_copy(
                    source.at[code - bases[i], :, pl.ds(col, buf.shape[2])], buf.at[k], sem
                ).start()

            if len(sources) == 1:
                start()
            else:
                inside = code >= bases[i]
                if i + 1 < len(sources):
                    inside = inside & (code < bases[i + 1])
                pl.when(inside)(start)
        return carry

    lax.fori_loop(0, buf.shape[0], one, 0, unroll=4 if buf.shape[0] % 4 == 0 else 1)


def gather_kernel(code_ref, *rest, cols, bases):
    *sources, out_ref, sem = rest
    fetch(code_ref, sources, cols, bases, out_ref, sem)
    pltpu.make_async_copy(out_ref, out_ref, sem).wait()


def gather(codes, sources, cols, bases, width):
    slot_len = sources[0].shape[1]
    shape = (codes.shape[0], slot_len, width)
    return pl.pallas_call(
        functools.partial(gather_kernel, cols=cols, bases=bases),
        grid_spec=pltpu.PrefetchScalarGridSpec(
            num_scalar_prefetch=1,
            grid=(1,),
            in_specs=[ANYWHERE] * len(sources),
            out_specs=pl.BlockSpec(shape, lambda i, *_: (0, 0, 0)),
            scratch_shapes=[pltpu.SemaphoreType.DMA],
        ),
        out_shape=jax.ShapeDtypeStruct(shape, sources[0].dtype),
        compiler_params=pltpu.CompilerParams(vmem_limit_bytes=16 << 20),
        cost_estimate=pl.CostEstimate(
            flops=0, transcendentals=0, bytes_accessed=4 * shape[0] * slot_len * width
        ),
        name="gather",
    )(codes, *sources)


def pack_kernel(code_ref, first_ref, pick_ref, *rest, cols, bases):
    *sources, k_ref, v_ref, buf, sem = rest
    kv_local, slot_len, window = k_ref.shape[0], buf.shape[1], pick_ref.shape[1]
    fetch(code_ref, sources, cols, bases, buf, sem)
    pltpu.make_async_copy(buf, buf, sem).wait()
    for ref in (k_ref, v_ref):
        ref[:, :DOC_MAX, :] = jnp.zeros((kv_local, DOC_MAX, HEAD_DIM), jnp.bfloat16)

    @pl.loop(0, pick_ref.shape[0] // TILE)
    def _(t):
        here = pl.multiple_of(t * TILE, TILE)
        rows = buf[pl.ds(first_ref[t], window // slot_len)].reshape(window, buf.shape[2])
        packed = jnp.dot(
            pick_ref[pl.ds(here, TILE), :], rows, preferred_element_type=jnp.float32
        ).astype(jnp.bfloat16)
        for n in range(2 * kv_local):
            ref = (k_ref, v_ref)[n // kv_local]
            ref[n % kv_local, pl.ds(DOC_MAX + here, TILE), :] = packed[
                :, n * HEAD_DIM : (n + 1) * HEAD_DIM
            ]


def pack(codes, first, pick, sources, cols, bases, kv_local):
    slot_len = sources[0].shape[1]
    shape = jax.ShapeDtypeStruct((kv_local, DOC_MAX + pick.shape[0], HEAD_DIM), jnp.bfloat16)
    return pl.pallas_call(
        functools.partial(pack_kernel, cols=cols, bases=bases),
        grid_spec=pltpu.PrefetchScalarGridSpec(
            num_scalar_prefetch=2,
            grid=(1,),
            in_specs=[WHOLE] + [ANYWHERE] * len(sources),
            out_specs=[WHOLE, WHOLE],
            scratch_shapes=[
                pltpu.VMEM((codes.shape[0], slot_len, 2 * kv_local * HEAD_DIM), jnp.bfloat16),
                pltpu.SemaphoreType.DMA,
            ],
        ),
        out_shape=[shape, shape],
        compiler_params=pltpu.CompilerParams(vmem_limit_bytes=16 << 20),
        name="pack",
    )(codes, first, pick, *sources)


def attend_kernel(code_ref, first_ref, k_ref, v_ref, pick_ref, bias_ref, *rest, cols, bases, heads):
    *sources, out_ref, q_buf, q_rows, sem = rest
    sources = sources[: len(cols)]
    tile = pl.program_id(0)
    slot_len, window = q_buf.shape[1], pick_ref.shape[1]
    span = bias_ref.shape[1]

    @pl.when(tile == 0)
    def _():
        fetch(code_ref, sources, cols, bases, q_buf, sem)
        pltpu.make_async_copy(q_buf, q_buf, sem).wait()

    here = pl.multiple_of(tile * TILE, TILE)
    pick = pick_ref[pl.ds(here, TILE), :]
    bias = bias_ref[pl.ds(here, TILE), :]
    live = jnp.max(bias, axis=1, keepdims=True) > -1.0
    keys = k_ref[pl.ds(here, span), :]
    values = v_ref[pl.ds(here, span), :]
    rows = q_buf[pl.ds(first_ref[tile], window // slot_len)].reshape(window, q_buf.shape[2])
    packed = jnp.dot(pick, rows, preferred_element_type=jnp.float32).astype(jnp.bfloat16)
    for h in range(heads):
        q_rows[h * TILE : (h + 1) * TILE, :] = packed[:, h * HEAD_DIM : (h + 1) * HEAD_DIM]
    scale = (HEAD_DIM**-0.5) * LOG2E
    stack = min(STACK, heads)
    for g in range(heads // stack):
        score = lax.dot_general(
            q_rows[g * stack * TILE : (g + 1) * stack * TILE, :],
            keys,
            (((1,), (1,)), ((), ())),
            preferred_element_type=jnp.float32,
        ).reshape(stack, TILE, span)
        score = score * scale + bias[None]
        peak = jnp.max(score, axis=2, keepdims=True)
        weight = jnp.exp2(score - peak)
        norm = jnp.sum(weight, axis=2, keepdims=True)
        mixed = jnp.dot(
            weight.astype(jnp.bfloat16).reshape(stack * TILE, span),
            values,
            preferred_element_type=jnp.float32,
        ).reshape(stack, TILE, HEAD_DIM)
        result = jnp.where(live[None], mixed / norm, 0.0).astype(jnp.bfloat16)
        for n in range(stack):
            h = g * stack + n
            out_ref[:, h * HEAD_DIM : (h + 1) * HEAD_DIM] = result[n]


def attend(codes, first, keys, values, pick, bias, sources, cols, bases, out, chunk, heads, kv_head, width):
    slot_len, (row_len, span) = sources[0].shape[1], bias.shape
    chunk_width = heads * HEAD_DIM
    one_head = pl.BlockSpec((None, DOC_MAX + row_len, HEAD_DIM), lambda t, *_: (kv_head, 0, 0))
    operands = [codes, first, keys, values, pick, bias, *sources]
    specs = [one_head, one_head, WHOLE, WHOLE] + [ANYWHERE] * len(sources)
    aliases = {}
    if out is not None:
        aliases = {len(operands): 0}
        operands.append(out)
        specs.append(ANYWHERE)
    return pl.pallas_call(
        functools.partial(attend_kernel, cols=cols, bases=bases, heads=heads),
        grid_spec=pltpu.PrefetchScalarGridSpec(
            num_scalar_prefetch=2,
            grid=(row_len // TILE,),
            in_specs=specs,
            out_specs=pl.BlockSpec((TILE, chunk_width), lambda t, *_: (t, chunk)),
            scratch_shapes=[
                pltpu.VMEM((codes.shape[0], slot_len, chunk_width), jnp.bfloat16),
                pltpu.VMEM((heads * TILE, HEAD_DIM), jnp.bfloat16),
                pltpu.SemaphoreType.DMA,
            ],
        ),
        out_shape=jax.ShapeDtypeStruct((row_len, width), jnp.bfloat16),
        input_output_aliases=aliases,
        compiler_params=pltpu.CompilerParams(vmem_limit_bytes=32 << 20),
        cost_estimate=pl.CostEstimate(
            flops=4 * row_len * span * chunk_width,
            transcendentals=row_len * span * heads,
            bytes_accessed=6 * row_len * chunk_width,
        ),
        name="attend",
    )(*operands)


def lists_of(masks, codes, slots):
    items = masks.shape[1]
    upto = jnp.arange(items)[:, None] <= jnp.arange(items)[None, :]
    rank = jnp.dot(
        masks.astype(jnp.bfloat16), upto.astype(jnp.bfloat16), preferred_element_type=jnp.float32
    ).astype(jnp.int32) - 1
    rank = jnp.where(masks, rank, -1)
    if codes is None:
        return rank
    at = rank[:, None, :] == jnp.arange(slots, dtype=jnp.int32)[None, :, None]
    return jnp.sum(jnp.where(at, codes, 0), axis=2)


def swap(rows, bit):
    pairs = [(i, i ^ bit) for i in range(lax.axis_size("dp"))]
    return lax.ppermute(rows, "dp", pairs)


MESH = pl.DeviceIdType.MESH


def meet_kernel(mine_ref, queries_ref, keys_ref, values_ref, table_ref, load_ref, count_ref, near_ref, *rest):
    kv_ref, send_sem, recv_sem = rest
    me, level = lax.axis_index("dp"), lax.axis_index("tensor")
    core = me & 1
    groups = table_ref.shape[0]
    half = queries_ref.shape[2] // 2
    barrier = pltpu.get_barrier_semaphore()
    for n in range(1, groups):
        pl.semaphore_signal(barrier, inc=1, device_id=(me ^ n, level), device_id_type=MESH)
    pl.semaphore_wait(barrier, groups - 1)
    copies = []
    for n in range(1, groups):
        copies.append(
            pltpu.make_async_remote_copy(
                mine_ref, table_ref.at[me], send_sem.at[n], recv_sem.at[n],
                device_id=(me ^ n, level), device_id_type=MESH,
            )
        )
    base = pl.multiple_of((core ^ 1) * half, HEAD_DIM)
    copies.append(
        pltpu.make_async_remote_copy(
            queries_ref.at[:, :, pl.ds(base, near_ref.shape[2])], near_ref, send_sem.at[0], recv_sem.at[0],
            device_id=(me ^ 1, level), device_id_type=MESH,
        )
    )
    for copy in copies:
        copy.start()
    table_ref[me] = mine_ref[...]
    for n in range(kv_ref.shape[0]):
        for part in range(2):
            head = pl.multiple_of((2 * n + (core ^ part)) * HEAD_DIM, HEAD_DIM)
            for kind, rows in enumerate((keys_ref, values_ref)):
                kv_ref[n, part, :, :, kind * HEAD_DIM : (kind + 1) * HEAD_DIM] = rows[:, :, pl.ds(head, HEAD_DIM)]
    for copy in copies[:-1]:
        copy.wait()
    dest, tokens = table_ref[:, 0, :], table_ref[:, 1, :]
    lane = lax.broadcasted_iota(jnp.int32, load_ref.shape, 1)
    load, count = jnp.zeros(load_ref.shape, jnp.int32), jnp.zeros(load_ref.shape, jnp.int32)
    for g in range(groups):
        load = jnp.where(lane == g, jnp.sum(jnp.where(dest == g, tokens, 0), axis=1, keepdims=True), load)
        count = jnp.where(lane == g, jnp.sum((dest == g).astype(jnp.int32), axis=1, keepdims=True), count)
    load_ref[...] = load
    count_ref[...] = count
    copies[-1].wait()


def meet(mine, queries, key_rows, value_rows, groups, ways, width):
    sentences, slot_len, _ = queries.shape
    bf16, i32 = jnp.bfloat16, jnp.int32
    small = jax.ShapeDtypeStruct((groups, groups), i32)
    kv = jax.ShapeDtypeStruct((ways, 2, key_rows.shape[0], slot_len, 2 * HEAD_DIM), bf16)
    return pl.pallas_call(
        meet_kernel,
        in_specs=[WHOLE, ANYWHERE, WHOLE, WHOLE],
        out_specs=[WHOLE, WHOLE, WHOLE, ANYWHERE, WHOLE],
        out_shape=[
            jax.ShapeDtypeStruct((groups, 2, sentences), i32), small, small,
            jax.ShapeDtypeStruct((sentences, slot_len, width), bf16),
            kv,
        ],
        scratch_shapes=[
            pltpu.SemaphoreType.DMA((groups,)),
            pltpu.SemaphoreType.DMA((groups,)),
        ],
        compiler_params=pltpu.CompilerParams(collective_id=0, has_side_effects=True),
        name="meet",
    )(mine, queries, key_rows, value_rows)


def plan_kernel(table_ref, load_ref, count_ref, plan_ref, tier_ref, slot_ref, begin_ref, shift_ref, key_ref, *, tiers):
    me = lax.axis_index("dp")
    chip, core = me >> 1, me & 1
    groups, _, sentences = table_ref.shape
    chips = groups // 2
    load = [[load_ref[2 * a, g] + load_ref[2 * a + 1, g] for g in range(groups)] for a in range(chips)]
    begin, totals = [[None] * groups for _ in range(chips)], [None] * groups
    for g in range(groups):
        total = jnp.int32(0)
        for a in range(chips):
            begin[a][g] = total
            total = total + load[a][g]
        totals[g] = total
    need = [jnp.int32(0)] * chips
    for a in range(chips):
        for b in range(chips):
            one = begin[a][2 * b] & (LEAST - 1)
            end = one + load[a][2 * b]
            two = end + ((begin[a][2 * b + 1] - end) & (LEAST - 1))
            need[a ^ b] = jnp.maximum(need[a ^ b], two + load[a][2 * b + 1])
            for g, first in ((2 * b, one), (2 * b + 1, two)):
                shift_ref[a * groups + g] = first
                begin_ref[a * groups + g] = begin[a][g]
    tier = jnp.int32(len(tiers) - 1)
    for n in reversed(range(len(tiers) - 1)):
        fits = functools.reduce(jnp.logical_and, [low <= cap for low, cap in zip(need, tiers[n])])
        tier = jnp.where(fits, n, tier)
    tier_ref[0] = tier
    passed = jnp.int32(0)
    for key in range(groups):
        group = key ^ (2 * chip)
        key_ref[key] = passed
        key_ref[groups + key] = shift_ref[chip * groups + group]
        for n in range(1, 16) if key % 2 else range(1):
            plan_ref[FIRST + 16 * (key // 2) + n] = passed
        passed = passed + count_ref[2 * chip, group] + count_ref[2 * chip + 1, group]
    for half in range(2):
        mine = sentences * (half ^ core)

        def place(n, carry, half=half, mine=mine):
            key = table_ref[2 * chip + half, 0, n] ^ (2 * chip)
            size = table_ref[2 * chip + half, 1, n]
            flow = key >> 1
            at, row = key_ref[key], key_ref[groups + key]
            plan_ref[CODE + at] = mine + n
            plan_ref[START + at] = flow * FAR + row
            plan_ref[COUNT + at] = size
            key_ref[key] = at + 1
            key_ref[groups + key] = row + size
            tile = ((row + SEND_TILE - 1) * 37450) >> 22
            plan_ref[FIRST + 16 * flow + jnp.where(tile * SEND_TILE < row + size, tile, 15)] = at
            return carry

        lax.fori_loop(0, sentences, place, 0, unroll=8)
    for order in range(2):
        group = 2 * chip + (core if order == 1 else 1 - core)
        for flow in range(chips):
            at = chip ^ flow
            plan_ref[INTO + 16 * order + flow] = begin_ref[at * groups + group]
            plan_ref[INTO + 16 * order + 4 + flow] = load_ref[2 * at, group] + load_ref[2 * at + 1, group]
            plan_ref[INTO + 16 * order + 8 + flow] = shift_ref[at * groups + group]
        plan_ref[INTO + 16 * order + 12] = begin_ref[(chips - 1) * groups + group] + (
            load_ref[2 * chips - 2, group] + load_ref[2 * chips - 1, group]
        )
    lane = lax.broadcasted_iota(jnp.int32, (1, HEAD_DIM), 1)
    token = lane % SLOT
    for r in range(slot_ref.shape[0]):
        start, size = jnp.zeros((1, HEAD_DIM), jnp.int32), jnp.zeros((1, HEAD_DIM), jnp.int32)
        for n in range(HEAD_DIM // SLOT):
            at = r * (HEAD_DIM // SLOT) + n
            start = jnp.where(lane // SLOT == n, plan_ref[START + at], start)
            size = jnp.where(lane // SLOT == n, plan_ref[COUNT + at], size)
        slot_ref[r : r + 1, :] = jnp.where(token < size, start + token, -1)


def make_plan(table, load, count, tiers):
    groups, _, sentences = table.shape
    cells = groups // 2 * groups
    return pl.pallas_call(
        functools.partial(plan_kernel, tiers=tiers),
        in_specs=[SCALARS] * 3,
        out_specs=[SCALARS, SCALARS, WHOLE],
        out_shape=[
            jax.ShapeDtypeStruct((PLAN,), jnp.int32),
            jax.ShapeDtypeStruct((1,), jnp.int32),
            jax.ShapeDtypeStruct((2 * sentences * SLOT // HEAD_DIM, HEAD_DIM), jnp.int32),
        ],
        scratch_shapes=[pltpu.SMEM((cells,), jnp.int32)] * 2 + [pltpu.SMEM((2 * groups,), jnp.int32)],
        name="plan",
    )(table, load, count)


def post_kernel(plan_ref, slot_ref, *rest, caps, fetch_one):
    sources, rest = rest[: -2 * len(caps) - 3], rest[-2 * len(caps) - 3 :]
    outs, (*tiles, buf, sem, out_sem) = rest[: len(caps)], rest[len(caps) :]
    slot_len, width = buf.shape[1:]

    def one(n, carry):
        fetch_one(plan_ref[CODE + n], sources, buf.at[n], sem)
        return carry

    lax.fori_loop(0, buf.shape[0], one, 0, unroll=4)
    pltpu.make_async_copy(buf, buf, sem).wait()
    per = HEAD_DIM // slot_len
    deep = SPREAD // per
    for flow, (cap, out) in enumerate(zip(caps, tiles)):

        def fill(tile, low, size, flow=flow, out=out):
            row = lax.broadcasted_iota(jnp.int32, (size, HEAD_DIM), 0) + (flow * FAR + low)
            first = jnp.minimum(plan_ref[FIRST + 16 * flow + tile] // per, slot_ref.shape[0] - deep)
            pick = jnp.concatenate(
                [
                    (row == slot_ref[pl.ds(first + n, 1), :]).astype(jnp.float32).astype(jnp.bfloat16)
                    for n in range(deep)
                ],
                axis=1,
            )
            rows = buf[pl.ds(first * per, SPREAD)].reshape(SPREAD * slot_len, width)
            out[pl.ds(low, size), :] = jnp.dot(pick, rows, preferred_element_type=jnp.float32).astype(
                jnp.bfloat16
            )

        whole = cap // SEND_TILE
        if whole <= UNROLLED:
            for tile in range(whole):
                fill(tile, tile * SEND_TILE, SEND_TILE)
        else:

            @pl.loop(0, whole)
            def _(tile, fill=fill):
                fill(tile, pl.multiple_of(tile * SEND_TILE, LEAST), SEND_TILE)

        left = cap % SEND_TILE
        if left:
            fill(whole, cap - left, left)
        pltpu.make_async_copy(out, outs[flow], out_sem.at[flow]).start()
    for flow, out in enumerate(tiles):
        pltpu.make_async_copy(out, outs[flow], out_sem.at[flow]).wait()


def post(plan, slots, sources, fetch_one, caps, count, slot_len, width):
    shapes = [jax.ShapeDtypeStruct((cap, width), jnp.bfloat16) for cap in caps]
    return pl.pallas_call(
        functools.partial(post_kernel, caps=caps, fetch_one=fetch_one),
        grid_spec=pltpu.PrefetchScalarGridSpec(
            num_scalar_prefetch=1,
            grid=(1,),
            in_specs=[WHOLE] + [FAR_OFF] * len(sources),
            out_specs=[FAR_OFF] * len(caps),
            scratch_shapes=[pltpu.VMEM(shape.shape, shape.dtype) for shape in shapes] + [
                pltpu.VMEM((count, slot_len, width), jnp.bfloat16),
                pltpu.SemaphoreType.DMA,
                pltpu.SemaphoreType.DMA((len(caps),)),
            ],
        ),
        out_shape=shapes,
        compiler_params=pltpu.CompilerParams(vmem_limit_bytes=VMEM),
        cost_estimate=pl.CostEstimate(
            flops=0,
            transcendentals=0,
            bytes_accessed=SMALL,
        ),
        name="post",
    )(plan, slots, *sources)


def lend_kernel(rows_ref, out_ref, send_sem, recv_sem, *, region):
    me, level = lax.axis_index("dp"), lax.axis_index("tensor")
    barrier = pltpu.get_barrier_semaphore()
    pl.semaphore_signal(barrier, inc=1, device_id=(me ^ 1, level), device_id_type=MESH)
    pl.semaphore_wait(barrier, 1)
    copy = pltpu.make_async_remote_copy(
        rows_ref.at[region((me & 1) ^ 1)] if region else rows_ref, out_ref, send_sem, recv_sem,
        device_id=(me ^ 1, level), device_id_type=MESH,
    )
    copy.start()
    copy.wait()


def lend(rows, shape, region, number):
    return pl.pallas_call(
        functools.partial(lend_kernel, region=region),
        in_specs=[ANYWHERE],
        out_specs=ANYWHERE,
        out_shape=jax.ShapeDtypeStruct(shape, rows.dtype),
        scratch_shapes=[pltpu.SemaphoreType.DMA] * 2,
        compiler_params=pltpu.CompilerParams(
            collective_id=number, has_side_effects=True, vmem_limit_bytes=4 << 20
        ),
        cost_estimate=pl.CostEstimate(flops=0, transcendentals=0, bytes_accessed=SMALL),
        name="lend",
    )(rows)


def sort_kernel(plan_ref, *rest, caps, lead):
    flows, (away, own_ref, buf, sem) = rest[: len(caps)], rest[len(caps) :]
    row_len, width = own_ref.shape[0] - lead, own_ref.shape[1]
    for f, (cap, flow) in enumerate(zip(caps, flows)):
        pltpu.make_async_copy(flow, buf.at[f, pl.ds(TILE, cap)], sem.at[f]).start()
    for f, cap in enumerate(caps):
        for low in (0, TILE + cap):
            buf[f, low : low + TILE, :] = jnp.zeros((TILE, width), jnp.bfloat16)
    if lead:
        for out in (away, own_ref):
            out[:lead, :] = jnp.zeros((lead, width), jnp.bfloat16)
    for f, (cap, flow) in enumerate(zip(caps, flows)):
        pltpu.make_async_copy(flow, buf.at[f, pl.ds(TILE, cap)], sem.at[f]).wait()
    row = lax.broadcasted_iota(jnp.int32, (TILE, HEAD_DIM), 0)

    def fill(order, out):
        @pl.loop(0, row_len // TILE)
        def _(t):
            here = pl.multiple_of(t * TILE, TILE)
            total = None
            for f, cap in enumerate(caps):
                begin = plan_ref[INTO + 16 * order + f] - here
                size = plan_ref[INTO + 16 * order + 4 + f]
                low = plan_ref[INTO + 16 * order + 8 + f] - begin + TILE
                low = pl.multiple_of(jnp.clip(low, 0, TILE + cap), LEAST)
                mask = ((row >= begin) & (row < begin + size)).astype(jnp.float32).astype(jnp.bfloat16)
                mask = jnp.concatenate([mask] * (width // HEAD_DIM), axis=1)
                part = buf[f, pl.ds(low, TILE), :] * mask
                total = part if total is None else total + part
            out[pl.ds(lead + here, TILE), :] = total

    fill(0, away)
    fill(1, own_ref)


def sort(plan, flows, row_len, lead):
    caps = tuple(flow.shape[0] for flow in flows)
    width = flows[0].shape[1]
    shape = jax.ShapeDtypeStruct((lead + row_len, width), jnp.bfloat16)
    return pl.pallas_call(
        functools.partial(sort_kernel, caps=caps, lead=lead),
        in_specs=[SCALARS] + [ANYWHERE] * len(flows),
        out_specs=[WHOLE, WHOLE],
        out_shape=[shape, shape],
        scratch_shapes=[
            pltpu.VMEM((len(caps), max(caps) + 2 * TILE, width), jnp.bfloat16),
            pltpu.SemaphoreType.DMA((len(caps),)),
        ],
        compiler_params=pltpu.CompilerParams(
            vmem_limit_bytes=VMEM if width > 1024 else 24 << 20,
        ),
        cost_estimate=pl.CostEstimate(flops=0, transcendentals=0, bytes_accessed=SMALL),
        name="sort",
    )(plan, *flows)


def mix_kernel(plan_ref, bias_ref, *rest, cols, half):
    pairs, (*_, out_ref, buf, sem) = rest[:4], rest[4:]
    tile, last = pl.program_id(0), pl.num_programs(0) - 1
    span = bias_ref.shape[1]
    width = pairs[0].shape[1]
    here = pl.multiple_of(tile * TILE, TILE)
    bias = bias_ref[...]
    live = jnp.max(bias, axis=1, keepdims=True) > -1.0
    scale = (HEAD_DIM**-0.5) * LOG2E
    stack = min(STACK, width // HEAD_DIM)
    core = lax.axis_index("dp") & 1
    turn = tile & 1

    def send(step, side, way):
        col = pl.multiple_of((core ^ side) * half + cols, HEAD_DIM)
        row = pl.multiple_of(step * TILE, TILE)
        copy = pltpu.make_async_copy(
            buf.at[step & 1, side], out_ref.at[pl.ds(row, TILE), pl.ds(col, width)], sem.at[step & 1, side]
        )
        copy.start() if way else copy.wait()

    @pl.when(tile >= 2)
    def _():
        for side in range(2):
            send(tile - 2, side, False)

    groups = []
    for side in range(2):
        q_ref, kv_ref = pairs[2 * side : 2 * side + 2]
        for g in range(width // HEAD_DIM // stack):
            groups.append((side, g, q_ref, kv_ref))

    def score_of(group):
        side, g, q_ref, kv_ref = group
        rows = jnp.concatenate(
            [q_ref[:, (g * stack + n) * HEAD_DIM : (g * stack + n + 1) * HEAD_DIM] for n in range(stack)],
            axis=0,
        )
        return lax.dot_general(
            rows, kv_ref[pl.ds(here, span), :HEAD_DIM], (((1,), (1,)), ((), ())),
            preferred_element_type=jnp.float32,
        ).reshape(stack, TILE, span)

    def finish(group, weight, norm):
        side, g, q_ref, kv_ref = group
        mixed = jnp.dot(
            weight, kv_ref[pl.ds(here, span), HEAD_DIM:], preferred_element_type=jnp.float32
        ).reshape(stack, TILE, HEAD_DIM)
        result = jnp.where(live[None], mixed / norm, 0.0).astype(jnp.bfloat16)
        for n in range(stack):
            h = g * stack + n
            buf[turn, side, :, h * HEAD_DIM : (h + 1) * HEAD_DIM] = result[n]

    following, held = score_of(groups[0]), None
    for n, group in enumerate(groups):
        score = following
        following = score_of(groups[n + 1]) if n + 1 < len(groups) else None
        score = score * scale + bias[None]
        peak = jnp.max(score, axis=2, keepdims=True)
        weight = jnp.exp2(score - peak)
        norm = jnp.sum(weight, axis=2, keepdims=True)
        if held is not None:
            finish(*held)
        held = group, weight.astype(jnp.bfloat16).reshape(stack * TILE, span), norm
    finish(*held)
    for side in range(2):
        send(tile, side, True)

    @pl.when(tile == last)
    def _():
        for side in range(2):
            send(tile - 1, side, False)
            send(tile, side, False)


def mix(plan, bias, own, far, out, full_width, col):
    (row_len, width), span = own[0].shape, bias.shape[1]
    operands = [plan, bias, *own, *far]
    rows = pl.BlockSpec((TILE, width), lambda t, *_: (t, 0))
    whole = pl.BlockSpec(own[1].shape, lambda t, *_: (0, 0))
    specs = [pl.BlockSpec((TILE, span), lambda t, *_: (t, 0)), rows, whole, rows, whole]
    aliases = {}
    if out is not None:
        aliases = {len(operands): 0}
        operands.append(out)
        specs.append(ANYWHERE)
    return pl.pallas_call(
        functools.partial(mix_kernel, cols=col, half=full_width // 2),
        grid_spec=pltpu.PrefetchScalarGridSpec(
            num_scalar_prefetch=1,
            grid=(row_len // TILE,),
            in_specs=specs,
            out_specs=ANYWHERE,
            scratch_shapes=[
                pltpu.VMEM((2, 2, TILE, width), jnp.bfloat16),
                pltpu.SemaphoreType.DMA((2, 2)),
            ],
        ),
        out_shape=jax.ShapeDtypeStruct((row_len, full_width), jnp.bfloat16),
        input_output_aliases=aliases,
        compiler_params=pltpu.CompilerParams(vmem_limit_bytes=32 << 20),
        cost_estimate=pl.CostEstimate(flops=0, transcendentals=0, bytes_accessed=SMALL),
        name="mix",
    )(*operands)


def after(value, *others):
    return lax.optimization_barrier((value, *others))[1:]


def eight_groups(queries, key_rows, value_rows, destination, token_count, doc_ids):
    ways = lax.axis_size("tensor")
    core = lax.axis_index("dp") & 1
    sentences, slot_len, q_width = queries.shape
    lanes = key_rows.shape[0]
    row_len = doc_ids.shape[1]
    half = q_width // 2
    kv_width = key_rows.shape[2] // ways
    full = 4 * (sentences // 4) * slot_len
    tiers = [(TIERS[-1], cap, cap, cap) for cap in TIERS] + [(full + 32,) * 4]
    def fetch_q(code, sources, into, sem, col, skip):
        own, near = sources
        width = into.shape[1]

        @pl.when(code < sentences)
        def _():
            base = pl.multiple_of((lax.axis_index("dp") & 1) * half + col, HEAD_DIM)
            pltpu.make_async_copy(own.at[code, :, pl.ds(base, width)], into, sem).start()

        @pl.when(code >= sentences)
        def _():
            pltpu.make_async_copy(
                near.at[code - sentences, :, pl.ds(col - skip, width)], into, sem
            ).start()

    def fetch_kv(code, sources, into, sem):
        own, near = sources
        from_level = (code & (sentences - 1)) // lanes
        lane = code & (lanes - 1)

        @pl.when(code < sentences)
        def _():
            pltpu.make_async_copy(own.at[from_level, 0, lane], into, sem).start()

        @pl.when(code >= sentences)
        def _():
            pltpu.make_async_copy(near.at[from_level, lane], into, sem).start()

    mine = jnp.stack([destination, token_count])
    table, load, number, near_first, kv = meet(
        mine, queries, key_rows, value_rows, lax.axis_size("dp"), ways, ROUNDS[0]
    )
    plan, tier, slots = make_plan(table, load, number, tiers)

    def with_caps(caps, widths, queries, near_first, plan, slots, doc_ids, kv):
        cols = [sum(widths[:n]) for n in range(len(widths))]
        rounds = len(widths)
        sent, arrived = [None] * rounds, [None] * rounds
        fresh = widths[0] != near_first.shape[2]
        skip = 0 if fresh else widths[0]

        def rest_of(core):
            start = pl.multiple_of(core * half + skip, HEAD_DIM)
            return slice(None), slice(None), pl.ds(start, half - skip)

        def others(core):
            return slice(None), 1

        def lend_rest(order):
            return lend(
                after(order, queries)[0], (sentences, slot_len, half - skip), rest_of, 4 if fresh else 1
            )

        def load(n, order):
            ready, base = (near_first, 0) if n == 0 and not fresh else (near, skip)
            sent[n] = post(
                order, slots, [queries, ready], functools.partial(fetch_q, col=cols[n], skip=base), caps,
                2 * sentences, slot_len, widths[n],
            )
            return after(sent[n][0], plan)[0]

        def depart(flows):
            far, beside, across = (swap(flows[f], 2 * f) for f in (3, 1, 2))
            return [flows[0], beside, across, far]

        if fresh:
            near = lend_rest(plan)
        order = load(0, plan)
        arrived[0] = depart(sent[0])
        if rounds > 1:
            near = lend_rest(order)
            order, = after(near, plan)
        if rounds > 1:
            order = load(1, order)
            order, *flows = after(arrived[0], order, *sent[1])
            arrived[1] = depart(flows)
        kv = lax.all_to_all(after(order, kv)[0], "tensor", split_axis=0, concat_axis=0, tiled=True)
        for n in range(2, rounds):
            order = load(n, order)
        docs, = after(order, doc_ids[0])

        live = jnp.arange(row_len, dtype=jnp.int32) < plan[INTO + 16 + 12]
        span = DOC_MAX + TILE
        padded = jnp.concatenate([jnp.full((DOC_MAX,), -1, jnp.int32), docs])
        tiles = row_len // TILE
        key_docs = jnp.stack([padded[t * TILE : t * TILE + span] for t in range(tiles)])
        col = jnp.arange(span, dtype=jnp.int32)[None, None, :]
        row = jnp.arange(TILE, dtype=jnp.int32)[None, :, None]
        allowed = (
            (col - DOC_MAX <= row)
            & (key_docs[:, None, :] == docs.reshape(tiles, TILE)[:, :, None])
            & live.reshape(tiles, TILE)[:, :, None]
        )
        bias = jnp.where(allowed, 0.0, NEG).astype(jnp.float32).reshape(row_len, span)

        order, kv = after(bias, order, kv)
        steps = list(range(rounds))
        kv_turn = min(3, rounds)
        steps.insert(kv_turn, None)
        out, mixed = None, 0
        q_rows, kv_rows, kv_arrived = [None] * rounds, None, None

        def settle(step, order):
            nonlocal kv_rows
            if step is None:
                kv_away, kv_own = sort(order, kv_arrived, row_len, DOC_MAX)
                kv_rows = kv_own, lend(kv_away, kv_away.shape, None, 5)
                return after(kv_rows[1], plan)[0]
            q_away, q_own = sort(order, arrived[step], row_len, 0)
            q_far = lend(q_away, q_away.shape, None, 5 + sorted({*ROUNDS, half}).index(widths[step]) + 1)
            q_rows[step] = q_own, q_far
            return after(q_far, plan)[0]

        def load_kv(order):
            near_kv = lend(after(order, kv)[0], kv.shape[:1] + kv.shape[2:], others, 2)
            flows = post(
                order, slots, [kv, near_kv], fetch_kv, caps, 2 * sentences, slot_len, 2 * HEAD_DIM
            )
            return flows, after(flows[0], plan)[0]

        kv_sent = None
        for at in range(len(steps)):
            if at + 1 < len(steps):
                step = steps[at + 1]
                if step is None:
                    if kv_sent is None:
                        kv_sent, order = load_kv(order)
                    flows = kv_sent
                else:
                    flows = sent[step]
                here = kv_arrived if steps[at] is None else arrived[steps[at]]
                if step is None or arrived[step] is None:
                    order, *flows = after(here, order, *flows)
                    flows = depart(flows)
                    if step is None:
                        kv_arrived = flows
                    else:
                        arrived[step] = flows
            order = settle(steps[at], order)
            while kv_rows is not None and mixed < rounds and q_rows[mixed] is not None:
                q_own, q_far = q_rows[mixed]
                out = mix(
                    order, bias, (q_own, kv_rows[0]), (q_far, kv_rows[1]), out, q_width, cols[mixed]
                )
                order, = after(out, plan)
                mixed += 1
        return out

    return lax.switch(
        tier[0],
        [functools.partial(with_caps, caps, ROUNDS) for caps in tiers[:-1]]
        + [functools.partial(with_caps, tiers[-1], (half,))],
        queries, near_first, plan, slots, doc_ids, kv,
    )


def per_device(queries, key_rows, value_rows, destination, token_count, doc_ids):
    groups = lax.axis_size("dp")
    ways = lax.axis_size("tensor")
    me = lax.axis_index("dp")
    sentences = destination.shape[0]
    slot_len = queries.shape[1]
    row_len = doc_ids.shape[1]
    q_width = queries.shape[2]
    kv_width = key_rows.shape[2] // ways
    kv_local = kv_width // HEAD_DIM
    per_group = q_width // kv_width
    heads = min(CHUNK_HEADS, per_group)
    chunk_width = heads * HEAD_DIM

    if groups == 8:
        return eight_groups(queries, key_rows, value_rows, destination, token_count, doc_ids)

    table = lax.all_gather(jnp.stack([destination, token_count]), "dp", axis=0)

    def split(rows):
        return rows.reshape(rows.shape[0], slot_len, ways, kv_width)

    def own_heads(key_rows, value_rows):
        kv = jnp.concatenate([split(key_rows), split(value_rows)], axis=3)
        return lax.all_to_all(
            jnp.transpose(kv, (2, 0, 1, 3)), "tensor", split_axis=0, concat_axis=0, tiled=True
        ).reshape(sentences, slot_len, 2 * kv_width)

    dest = table[:, 0, :].reshape(-1)
    counts = table[:, 1, :].reshape(-1)
    source = jnp.repeat(jnp.arange(groups, dtype=jnp.int32), sentences)
    lane = jnp.tile(jnp.arange(sentences, dtype=jnp.int32), groups)

    count_of = lists_of((dest == me)[None], counts[None, None, :], sentences)[0]
    nth = jnp.arange(sentences, dtype=jnp.int32)
    ends = jnp.sum(jnp.where(nth[None, :] <= nth[:, None], count_of[None, :], 0), axis=1)
    place = jnp.arange(row_len, dtype=jnp.int32)
    passed = place[:, None] >= ends[None, :]
    which = jnp.sum(passed.astype(jnp.int32), axis=1)
    start = jnp.sum(jnp.where(passed, count_of[None, :], 0), axis=1)
    live = which < sentences
    spread = min(sentences, (TILE - 1 + LEAST - 1) // LEAST + 1)
    heads_of = place[::TILE]
    first = jnp.sum((heads_of[:, None] >= ends[None, :]).astype(jnp.int32), axis=1)
    first = jnp.minimum(first, sentences - spread)
    window = spread * slot_len
    relative = (which - jnp.repeat(first, TILE)) * slot_len + place - start
    pick = (
        live[:, None] & (relative[:, None] == jnp.arange(window, dtype=jnp.int32)[None, :])
    ).astype(jnp.bfloat16)
    span = DOC_MAX + TILE
    padded = jnp.concatenate([jnp.full((DOC_MAX,), -1, jnp.int32), doc_ids[0]])
    tiles = row_len // TILE
    key_docs = jnp.stack([padded[t * TILE : t * TILE + span] for t in range(tiles)])
    col = jnp.arange(span, dtype=jnp.int32)[None, None, :]
    row = jnp.arange(TILE, dtype=jnp.int32)[None, :, None]
    allowed = (
        (col - DOC_MAX <= row)
        & (key_docs[:, None, :] == doc_ids[0].reshape(tiles, TILE)[:, :, None])
        & live.reshape(tiles, TILE)[:, :, None]
    )
    bias = jnp.where(allowed, 0.0, NEG).astype(jnp.float32).reshape(row_len, span)

    chunks = q_width // chunk_width

    def attend_one(chunk, kv_packed, first, got, codes, out):
        return attend(
            codes, first, *kv_packed, pick, bias, *got, out, chunk, heads, chunk * heads // per_group, q_width
        )

    capacity = max(2, (2 * sentences + groups - 1) // groups)
    rank = lists_of(destination[None, :] == jnp.arange(groups, dtype=jnp.int32)[:, None], None, None)
    slot = jnp.arange(capacity, dtype=jnp.int32)
    at = rank[:, None, :] == slot[None, :, None]
    picked = jnp.sum(jnp.where(at, nth[None, None, :], 0), axis=2).reshape(-1)
    by_source = (dest == me).reshape(groups, sentences)
    rank_in = lists_of(by_source, None, None).reshape(-1)
    codes = lists_of(
        (dest == me)[None], (source * capacity + rank_in)[None, None, :], sentences
    )[0]

    def exchange(rows, col, width):
        sent = gather(picked, [rows], (col,), (0,), width)
        got = lax.all_to_all(sent, "dp", split_axis=0, concat_axis=0, tiled=True)
        return [got], (0,), (0,)

    got_kv = exchange(own_heads(key_rows, value_rows), 0, 2 * kv_width)
    got_q = [exchange(queries, n * chunk_width, chunk_width) for n in range(chunks)]
    kv_packed = pack(codes, first, pick, *got_kv, kv_local)
    out = None
    for n in range(chunks):
        out = attend_one(n, kv_packed, first, got_q[n], codes, out)
    return out


def solution(mesh):
    placed = (
        P("dp", None, "tensor"),
        P(("dp", "tensor"), None, None),
        P(("dp", "tensor"), None, None),
        P("dp"),
        P("dp"),
        P("dp", None),
    )
    return jax.shard_map(
        per_device, mesh=mesh, in_specs=placed, out_specs=P("dp", "tensor"), check_vma=False
    )
```

```python
import functools
import jax
import jax.numpy as jnp
from jax import lax
from jax.experimental import pallas as pl
from jax.experimental.pallas import tpu as pltpu
from jax.sharding import PartitionSpec as P

HEAD_DIM = 128
DOC_MAX = 256
LEAST = 16
TILE = 128
CHUNK_HEADS = 8
STACK = 4
SEND_TILE = 112
SPREAD = 12
SLOT = 32
SMALL = 1
UNROLLED = 8
VMEM = 56 << 20
ROUNDS = (512, 512, 512, 256, 256)
TIERS = (528, 592, 688)
FAR = 1 << 20
CODE, START, COUNT, FIRST, INTO, TIER, PLAN = 0, 64, 128, 192, 256, 320, 336
NEG = -1e30
LOG2E = 1.4426950408889634
WHOLE = pl.BlockSpec(memory_space=pltpu.VMEM)
ANYWHERE = pl.BlockSpec(memory_space=pl.ANY)
FAR_OFF = pl.BlockSpec(memory_space=pltpu.HBM)
SCALARS = pl.BlockSpec(memory_space=pltpu.SMEM)


def fetch(code_ref, sources, cols, bases, buf, sem):
    def one(k, carry):
        code = code_ref[k]
        for i, (source, col) in enumerate(zip(sources, cols)):

            def start(i=i, source=source, col=col):
                pltpu.make_async_copy(
                    source.at[code - bases[i], :, pl.ds(col, buf.shape[2])], buf.at[k], sem
                ).start()

            if len(sources) == 1:
                start()
            else:
                inside = code >= bases[i]
                if i + 1 < len(sources):
                    inside = inside & (code < bases[i + 1])
                pl.when(inside)(start)
        return carry

    lax.fori_loop(0, buf.shape[0], one, 0, unroll=4 if buf.shape[0] % 4 == 0 else 1)


def gather_kernel(code_ref, *rest, cols, bases):
    *sources, out_ref, sem = rest
    fetch(code_ref, sources, cols, bases, out_ref, sem)
    pltpu.make_async_copy(out_ref, out_ref, sem).wait()


def gather(codes, sources, cols, bases, width):
    slot_len = sources[0].shape[1]
    shape = (codes.shape[0], slot_len, width)
    return pl.pallas_call(
        functools.partial(gather_kernel, cols=cols, bases=bases),
        grid_spec=pltpu.PrefetchScalarGridSpec(
            num_scalar_prefetch=1,
            grid=(1,),
            in_specs=[ANYWHERE] * len(sources),
            out_specs=pl.BlockSpec(shape, lambda i, *_: (0, 0, 0)),
            scratch_shapes=[pltpu.SemaphoreType.DMA],
        ),
        out_shape=jax.ShapeDtypeStruct(shape, sources[0].dtype),
        compiler_params=pltpu.CompilerParams(vmem_limit_bytes=16 << 20),
        cost_estimate=pl.CostEstimate(
            flops=0, transcendentals=0, bytes_accessed=4 * shape[0] * slot_len * width
        ),
        name="gather",
    )(codes, *sources)


def pack_kernel(code_ref, first_ref, pick_ref, *rest, cols, bases):
    *sources, k_ref, v_ref, buf, sem = rest
    kv_local, slot_len, window = k_ref.shape[0], buf.shape[1], pick_ref.shape[1]
    fetch(code_ref, sources, cols, bases, buf, sem)
    pltpu.make_async_copy(buf, buf, sem).wait()
    for ref in (k_ref, v_ref):
        ref[:, :DOC_MAX, :] = jnp.zeros((kv_local, DOC_MAX, HEAD_DIM), jnp.bfloat16)

    @pl.loop(0, pick_ref.shape[0] // TILE)
    def _(t):
        here = pl.multiple_of(t * TILE, TILE)
        rows = buf[pl.ds(first_ref[t], window // slot_len)].reshape(window, buf.shape[2])
        packed = jnp.dot(
            pick_ref[pl.ds(here, TILE), :], rows, preferred_element_type=jnp.float32
        ).astype(jnp.bfloat16)
        for n in range(2 * kv_local):
            ref = (k_ref, v_ref)[n // kv_local]
            ref[n % kv_local, pl.ds(DOC_MAX + here, TILE), :] = packed[
                :, n * HEAD_DIM : (n + 1) * HEAD_DIM
            ]


def pack(codes, first, pick, sources, cols, bases, kv_local):
    slot_len = sources[0].shape[1]
    shape = jax.ShapeDtypeStruct((kv_local, DOC_MAX + pick.shape[0], HEAD_DIM), jnp.bfloat16)
    return pl.pallas_call(
        functools.partial(pack_kernel, cols=cols, bases=bases),
        grid_spec=pltpu.PrefetchScalarGridSpec(
            num_scalar_prefetch=2,
            grid=(1,),
            in_specs=[WHOLE] + [ANYWHERE] * len(sources),
            out_specs=[WHOLE, WHOLE],
            scratch_shapes=[
                pltpu.VMEM((codes.shape[0], slot_len, 2 * kv_local * HEAD_DIM), jnp.bfloat16),
                pltpu.SemaphoreType.DMA,
            ],
        ),
        out_shape=[shape, shape],
        compiler_params=pltpu.CompilerParams(vmem_limit_bytes=16 << 20),
        name="pack",
    )(codes, first, pick, *sources)


def attend_kernel(code_ref, first_ref, k_ref, v_ref, pick_ref, bias_ref, *rest, cols, bases, heads):
    *sources, out_ref, q_buf, q_rows, sem = rest
    sources = sources[: len(cols)]
    tile = pl.program_id(0)
    slot_len, window = q_buf.shape[1], pick_ref.shape[1]
    span = bias_ref.shape[1]

    @pl.when(tile == 0)
    def _():
        fetch(code_ref, sources, cols, bases, q_buf, sem)
        pltpu.make_async_copy(q_buf, q_buf, sem).wait()

    here = pl.multiple_of(tile * TILE, TILE)
    pick = pick_ref[pl.ds(here, TILE), :]
    bias = bias_ref[pl.ds(here, TILE), :]
    live = jnp.max(bias, axis=1, keepdims=True) > -1.0
    keys = k_ref[pl.ds(here, span), :]
    values = v_ref[pl.ds(here, span), :]
    rows = q_buf[pl.ds(first_ref[tile], window // slot_len)].reshape(window, q_buf.shape[2])
    packed = jnp.dot(pick, rows, preferred_element_type=jnp.float32).astype(jnp.bfloat16)
    for h in range(heads):
        q_rows[h * TILE : (h + 1) * TILE, :] = packed[:, h * HEAD_DIM : (h + 1) * HEAD_DIM]
    scale = (HEAD_DIM**-0.5) * LOG2E
    stack = min(STACK, heads)
    for g in range(heads // stack):
        score = lax.dot_general(
            q_rows[g * stack * TILE : (g + 1) * stack * TILE, :],
            keys,
            (((1,), (1,)), ((), ())),
            preferred_element_type=jnp.float32,
        ).reshape(stack, TILE, span)
        score = score * scale + bias[None]
        peak = jnp.max(score, axis=2, keepdims=True)
        weight = jnp.exp2(score - peak)
        norm = jnp.sum(weight, axis=2, keepdims=True)
        mixed = jnp.dot(
            weight.astype(jnp.bfloat16).reshape(stack * TILE, span),
            values,
            preferred_element_type=jnp.float32,
        ).reshape(stack, TILE, HEAD_DIM)
        result = jnp.where(live[None], mixed / norm, 0.0).astype(jnp.bfloat16)
        for n in range(stack):
            h = g * stack + n
            out_ref[:, h * HEAD_DIM : (h + 1) * HEAD_DIM] = result[n]


def attend(codes, first, keys, values, pick, bias, sources, cols, bases, out, chunk, heads, kv_head, width):
    slot_len, (row_len, span) = sources[0].shape[1], bias.shape
    chunk_width = heads * HEAD_DIM
    one_head = pl.BlockSpec((None, DOC_MAX + row_len, HEAD_DIM), lambda t, *_: (kv_head, 0, 0))
    operands = [codes, first, keys, values, pick, bias, *sources]
    specs = [one_head, one_head, WHOLE, WHOLE] + [ANYWHERE] * len(sources)
    aliases = {}
    if out is not None:
        aliases = {len(operands): 0}
        operands.append(out)
        specs.append(ANYWHERE)
    return pl.pallas_call(
        functools.partial(attend_kernel, cols=cols, bases=bases, heads=heads),
        grid_spec=pltpu.PrefetchScalarGridSpec(
            num_scalar_prefetch=2,
            grid=(row_len // TILE,),
            in_specs=specs,
            out_specs=pl.BlockSpec((TILE, chunk_width), lambda t, *_: (t, chunk)),
            scratch_shapes=[
                pltpu.VMEM((codes.shape[0], slot_len, chunk_width), jnp.bfloat16),
                pltpu.VMEM((heads * TILE, HEAD_DIM), jnp.bfloat16),
                pltpu.SemaphoreType.DMA,
            ],
        ),
        out_shape=jax.ShapeDtypeStruct((row_len, width), jnp.bfloat16),
        input_output_aliases=aliases,
        compiler_params=pltpu.CompilerParams(vmem_limit_bytes=32 << 20),
        cost_estimate=pl.CostEstimate(
            flops=4 * row_len * span * chunk_width,
            transcendentals=row_len * span * heads,
            bytes_accessed=6 * row_len * chunk_width,
        ),
        name="attend",
    )(*operands)


def lists_of(masks, codes, slots):
    items = masks.shape[1]
    upto = jnp.arange(items)[:, None] <= jnp.arange(items)[None, :]
    rank = jnp.dot(
        masks.astype(jnp.bfloat16), upto.astype(jnp.bfloat16), preferred_element_type=jnp.float32
    ).astype(jnp.int32) - 1
    rank = jnp.where(masks, rank, -1)
    if codes is None:
        return rank
    at = rank[:, None, :] == jnp.arange(slots, dtype=jnp.int32)[None, :, None]
    return jnp.sum(jnp.where(at, codes, 0), axis=2)


def swap(rows, bit):
    pairs = [(i, i ^ bit) for i in range(lax.axis_size("dp"))]
    return lax.ppermute(rows, "dp", pairs)


MESH = pl.DeviceIdType.MESH


def meet_kernel(mine_ref, queries_ref, keys_ref, values_ref, table_ref, load_ref, count_ref, near_ref, *rest):
    kv_ref, send_sem, recv_sem = rest
    me, level = lax.axis_index("dp"), lax.axis_index("tensor")
    core = me & 1
    groups = table_ref.shape[0]
    half = queries_ref.shape[2] // 2
    barrier = pltpu.get_barrier_semaphore()
    for n in range(1, groups):
        pl.semaphore_signal(barrier, inc=1, device_id=(me ^ n, level), device_id_type=MESH)
    pl.semaphore_wait(barrier, groups - 1)
    copies = []
    for n in range(1, groups):
        copies.append(
            pltpu.make_async_remote_copy(
                mine_ref, table_ref.at[me], send_sem.at[n], recv_sem.at[n],
                device_id=(me ^ n, level), device_id_type=MESH,
            )
        )
    base = pl.multiple_of((core ^ 1) * half, HEAD_DIM)
    copies.append(
        pltpu.make_async_remote_copy(
            queries_ref.at[:, :, pl.ds(base, near_ref.shape[2])], near_ref, send_sem.at[0], recv_sem.at[0],
            device_id=(me ^ 1, level), device_id_type=MESH,
        )
    )
    for copy in copies:
        copy.start()
    table_ref[me] = mine_ref[...]
    for n in range(kv_ref.shape[0]):
        for part in range(2):
            head = pl.multiple_of((2 * n + (core ^ part)) * HEAD_DIM, HEAD_DIM)
            for kind, rows in enumerate((keys_ref, values_ref)):
                kv_ref[n, part, :, :, kind * HEAD_DIM : (kind + 1) * HEAD_DIM] = rows[:, :, pl.ds(head, HEAD_DIM)]
    for copy in copies[:-1]:
        copy.wait()
    dest, tokens = table_ref[:, 0, :], table_ref[:, 1, :]
    lane = lax.broadcasted_iota(jnp.int32, load_ref.shape, 1)
    load, count = jnp.zeros(load_ref.shape, jnp.int32), jnp.zeros(load_ref.shape, jnp.int32)
    for g in range(groups):
        load = jnp.where(lane == g, jnp.sum(jnp.where(dest == g, tokens, 0), axis=1, keepdims=True), load)
        count = jnp.where(lane == g, jnp.sum((dest == g).astype(jnp.int32), axis=1, keepdims=True), count)
    load_ref[...] = load
    count_ref[...] = count
    copies[-1].wait()


def meet(mine, queries, key_rows, value_rows, groups, ways, width):
    sentences, slot_len, _ = queries.shape
    bf16, i32 = jnp.bfloat16, jnp.int32
    small = jax.ShapeDtypeStruct((groups, groups), i32)
    kv = jax.ShapeDtypeStruct((ways, 2, key_rows.shape[0], slot_len, 2 * HEAD_DIM), bf16)
    return pl.pallas_call(
        meet_kernel,
        in_specs=[WHOLE, ANYWHERE, WHOLE, WHOLE],
        out_specs=[WHOLE, WHOLE, WHOLE, ANYWHERE, WHOLE],
        out_shape=[
            jax.ShapeDtypeStruct((groups, 2, sentences), i32), small, small,
            jax.ShapeDtypeStruct((sentences, slot_len, width), bf16),
            kv,
        ],
        scratch_shapes=[
            pltpu.SemaphoreType.DMA((groups,)),
            pltpu.SemaphoreType.DMA((groups,)),
        ],
        compiler_params=pltpu.CompilerParams(collective_id=0, has_side_effects=True),
        name="meet",
    )(mine, queries, key_rows, value_rows)


def plan_kernel(table_ref, load_ref, count_ref, plan_ref, tier_ref, slot_ref, begin_ref, shift_ref, key_ref, *, tiers):
    me = lax.axis_index("dp")
    chip, core = me >> 1, me & 1
    groups, _, sentences = table_ref.shape
    chips = groups // 2
    load = [[load_ref[2 * a, g] + load_ref[2 * a + 1, g] for g in range(groups)] for a in range(chips)]
    begin, totals = [[None] * groups for _ in range(chips)], [None] * groups
    for g in range(groups):
        total = jnp.int32(0)
        for a in range(chips):
            begin[a][g] = total
            total = total + load[a][g]
        totals[g] = total
    need = [jnp.int32(0)] * chips
    for a in range(chips):
        for b in range(chips):
            one = begin[a][2 * b] & (LEAST - 1)
            end = one + load[a][2 * b]
            two = end + ((begin[a][2 * b + 1] - end) & (LEAST - 1))
            need[a ^ b] = jnp.maximum(need[a ^ b], two + load[a][2 * b + 1])
            for g, first in ((2 * b, one), (2 * b + 1, two)):
                shift_ref[a * groups + g] = first
                begin_ref[a * groups + g] = begin[a][g]
    tier = jnp.int32(len(tiers) - 1)
    for n in reversed(range(len(tiers) - 1)):
        fits = functools.reduce(jnp.logical_and, [low <= cap for low, cap in zip(need, tiers[n])])
        tier = jnp.where(fits, n, tier)
    tier_ref[0] = tier
    passed = jnp.int32(0)
    for key in range(groups):
        group = key ^ (2 * chip)
        key_ref[key] = passed
        key_ref[groups + key] = shift_ref[chip * groups + group]
        for n in range(1, 16) if key % 2 else range(1):
            plan_ref[FIRST + 16 * (key // 2) + n] = passed
        passed = passed + count_ref[2 * chip, group] + count_ref[2 * chip + 1, group]
    for half in range(2):
        mine = sentences * (half ^ core)

        def place(n, carry, half=half, mine=mine):
            key = table_ref[2 * chip + half, 0, n] ^ (2 * chip)
            size = table_ref[2 * chip + half, 1, n]
            flow = key >> 1
            at, row = key_ref[key], key_ref[groups + key]
            plan_ref[CODE + at] = mine + n
            plan_ref[START + at] = flow * FAR + row
            plan_ref[COUNT + at] = size
            key_ref[key] = at + 1
            key_ref[groups + key] = row + size
            tile = ((row + SEND_TILE - 1) * 37450) >> 22
            plan_ref[FIRST + 16 * flow + jnp.where(tile * SEND_TILE < row + size, tile, 15)] = at
            return carry

        lax.fori_loop(0, sentences, place, 0, unroll=8)
    for order in range(2):
        group = 2 * chip + (core if order == 1 else 1 - core)
        for flow in range(chips):
            at = chip ^ flow
            plan_ref[INTO + 16 * order + flow] = begin_ref[at * groups + group]
            plan_ref[INTO + 16 * order + 4 + flow] = load_ref[2 * at, group] + load_ref[2 * at + 1, group]
            plan_ref[INTO + 16 * order + 8 + flow] = shift_ref[at * groups + group]
        plan_ref[INTO + 16 * order + 12] = begin_ref[(chips - 1) * groups + group] + (
            load_ref[2 * chips - 2, group] + load_ref[2 * chips - 1, group]
        )
    lane = lax.broadcasted_iota(jnp.int32, (1, HEAD_DIM), 1)
    token = lane % SLOT
    for r in range(slot_ref.shape[0]):
        start, size = jnp.zeros((1, HEAD_DIM), jnp.int32), jnp.zeros((1, HEAD_DIM), jnp.int32)
        for n in range(HEAD_DIM // SLOT):
            at = r * (HEAD_DIM // SLOT) + n
            start = jnp.where(lane // SLOT == n, plan_ref[START + at], start)
            size = jnp.where(lane // SLOT == n, plan_ref[COUNT + at], size)
        slot_ref[r : r + 1, :] = jnp.where(token < size, start + token, -1)


def make_plan(table, load, count, tiers):
    groups, _, sentences = table.shape
    cells = groups // 2 * groups
    return pl.pallas_call(
        functools.partial(plan_kernel, tiers=tiers),
        in_specs=[SCALARS] * 3,
        out_specs=[SCALARS, SCALARS, WHOLE],
        out_shape=[
            jax.ShapeDtypeStruct((PLAN,), jnp.int32),
            jax.ShapeDtypeStruct((1,), jnp.int32),
            jax.ShapeDtypeStruct((2 * sentences * SLOT // HEAD_DIM, HEAD_DIM), jnp.int32),
        ],
        scratch_shapes=[pltpu.SMEM((cells,), jnp.int32)] * 2 + [pltpu.SMEM((2 * groups,), jnp.int32)],
        name="plan",
    )(table, load, count)


def post_kernel(plan_ref, slot_ref, *rest, caps, fetch_one):
    sources, rest = rest[: -2 * len(caps) - 3], rest[-2 * len(caps) - 3 :]
    outs, (*tiles, buf, sem, out_sem) = rest[: len(caps)], rest[len(caps) :]
    slot_len, width = buf.shape[1:]

    def one(n, carry):
        fetch_one(plan_ref[CODE + n], sources, buf.at[n], sem)
        return carry

    lax.fori_loop(0, buf.shape[0], one, 0, unroll=4)
    pltpu.make_async_copy(buf, buf, sem).wait()
    per = HEAD_DIM // slot_len
    deep = SPREAD // per
    for flow, (cap, out) in enumerate(zip(caps, tiles)):

        def fill(tile, low, size, flow=flow, out=out):
            row = lax.broadcasted_iota(jnp.int32, (size, HEAD_DIM), 0) + (flow * FAR + low)
            first = jnp.minimum(plan_ref[FIRST + 16 * flow + tile] // per, slot_ref.shape[0] - deep)
            pick = jnp.concatenate(
                [
                    (row == slot_ref[pl.ds(first + n, 1), :]).astype(jnp.float32).astype(jnp.bfloat16)
                    for n in range(deep)
                ],
                axis=1,
            )
            rows = buf[pl.ds(first * per, SPREAD)].reshape(SPREAD * slot_len, width)
            out[pl.ds(low, size), :] = jnp.dot(pick, rows, preferred_element_type=jnp.float32).astype(
                jnp.bfloat16
            )

        whole = cap // SEND_TILE
        if whole <= UNROLLED:
            for tile in range(whole):
                fill(tile, tile * SEND_TILE, SEND_TILE)
        else:

            @pl.loop(0, whole)
            def _(tile, fill=fill):
                fill(tile, pl.multiple_of(tile * SEND_TILE, LEAST), SEND_TILE)

        left = cap % SEND_TILE
        if left:
            fill(whole, cap - left, left)
        pltpu.make_async_copy(out, outs[flow], out_sem.at[flow]).start()
    for flow, out in enumerate(tiles):
        pltpu.make_async_copy(out, outs[flow], out_sem.at[flow]).wait()


def post(plan, slots, sources, fetch_one, caps, count, slot_len, width):
    shapes = [jax.ShapeDtypeStruct((cap, width), jnp.bfloat16) for cap in caps]
    return pl.pallas_call(
        functools.partial(post_kernel, caps=caps, fetch_one=fetch_one),
        grid_spec=pltpu.PrefetchScalarGridSpec(
            num_scalar_prefetch=1,
            grid=(1,),
            in_specs=[WHOLE] + [FAR_OFF] * len(sources),
            out_specs=[FAR_OFF] * len(caps),
            scratch_shapes=[pltpu.VMEM(shape.shape, shape.dtype) for shape in shapes] + [
                pltpu.VMEM((count, slot_len, width), jnp.bfloat16),
                pltpu.SemaphoreType.DMA,
                pltpu.SemaphoreType.DMA((len(caps),)),
            ],
        ),
        out_shape=shapes,
        compiler_params=pltpu.CompilerParams(vmem_limit_bytes=VMEM),
        cost_estimate=pl.CostEstimate(
            flops=0,
            transcendentals=0,
            bytes_accessed=SMALL,
        ),
        name="post",
    )(plan, slots, *sources)


def lend_kernel(rows_ref, out_ref, send_sem, recv_sem, *, region):
    me, level = lax.axis_index("dp"), lax.axis_index("tensor")
    barrier = pltpu.get_barrier_semaphore()
    pl.semaphore_signal(barrier, inc=1, device_id=(me ^ 1, level), device_id_type=MESH)
    pl.semaphore_wait(barrier, 1)
    copy = pltpu.make_async_remote_copy(
        rows_ref.at[region((me & 1) ^ 1)] if region else rows_ref, out_ref, send_sem, recv_sem,
        device_id=(me ^ 1, level), device_id_type=MESH,
    )
    copy.start()
    copy.wait()


def lend(rows, shape, region, number):
    return pl.pallas_call(
        functools.partial(lend_kernel, region=region),
        in_specs=[ANYWHERE],
        out_specs=ANYWHERE,
        out_shape=jax.ShapeDtypeStruct(shape, rows.dtype),
        scratch_shapes=[pltpu.SemaphoreType.DMA] * 2,
        compiler_params=pltpu.CompilerParams(
            collective_id=number, has_side_effects=True, vmem_limit_bytes=4 << 20
        ),
        cost_estimate=pl.CostEstimate(flops=0, transcendentals=0, bytes_accessed=SMALL),
        name="lend",
    )(rows)


def sort_kernel(plan_ref, *rest, caps, lead):
    flows, (away, own_ref, buf, sem) = rest[: len(caps)], rest[len(caps) :]
    row_len, width = own_ref.shape[0] - lead, own_ref.shape[1]
    for f, (cap, flow) in enumerate(zip(caps, flows)):
        pltpu.make_async_copy(flow, buf.at[f, pl.ds(TILE, cap)], sem.at[f]).start()
    for f, cap in enumerate(caps):
        for low in (0, TILE + cap):
            buf[f, low : low + TILE, :] = jnp.zeros((TILE, width), jnp.bfloat16)
    if lead:
        for out in (away, own_ref):
            out[:lead, :] = jnp.zeros((lead, width), jnp.bfloat16)
    for f, (cap, flow) in enumerate(zip(caps, flows)):
        pltpu.make_async_copy(flow, buf.at[f, pl.ds(TILE, cap)], sem.at[f]).wait()
    row = lax.broadcasted_iota(jnp.int32, (TILE, HEAD_DIM), 0)

    def fill(order, out):
        @pl.loop(0, row_len // TILE)
        def _(t):
            here = pl.multiple_of(t * TILE, TILE)
            total = None
            for f, cap in enumerate(caps):
                begin = plan_ref[INTO + 16 * order + f] - here
                size = plan_ref[INTO + 16 * order + 4 + f]
                low = plan_ref[INTO + 16 * order + 8 + f] - begin + TILE
                low = pl.multiple_of(jnp.clip(low, 0, TILE + cap), LEAST)
                mask = ((row >= begin) & (row < begin + size)).astype(jnp.float32).astype(jnp.bfloat16)
                mask = jnp.concatenate([mask] * (width // HEAD_DIM), axis=1)
                part = buf[f, pl.ds(low, TILE), :] * mask
                total = part if total is None else total + part
            out[pl.ds(lead + here, TILE), :] = total

    fill(0, away)
    fill(1, own_ref)


def sort(plan, flows, row_len, lead):
    caps = tuple(flow.shape[0] for flow in flows)
    width = flows[0].shape[1]
    shape = jax.ShapeDtypeStruct((lead + row_len, width), jnp.bfloat16)
    return pl.pallas_call(
        functools.partial(sort_kernel, caps=caps, lead=lead),
        in_specs=[SCALARS] + [ANYWHERE] * len(flows),
        out_specs=[WHOLE, WHOLE],
        out_shape=[shape, shape],
        scratch_shapes=[
            pltpu.VMEM((len(caps), max(caps) + 2 * TILE, width), jnp.bfloat16),
            pltpu.SemaphoreType.DMA((len(caps),)),
        ],
        compiler_params=pltpu.CompilerParams(
            vmem_limit_bytes=VMEM if width > 1024 else 24 << 20,
        ),
        cost_estimate=pl.CostEstimate(flops=0, transcendentals=0, bytes_accessed=SMALL),
        name="sort",
    )(plan, *flows)


def mix_kernel(plan_ref, bias_ref, *rest, cols, half):
    pairs, (*_, out_ref, buf, sem) = rest[:4], rest[4:]
    tile, last = pl.program_id(0), pl.num_programs(0) - 1
    span = bias_ref.shape[1]
    width = pairs[0].shape[1]
    step_rows = buf.shape[2]
    bias = [bias_ref[low : low + TILE, :] for low in range(0, step_rows, TILE)]
    live = [jnp.max(one, axis=1, keepdims=True) > -1.0 for one in bias]
    scale = (HEAD_DIM**-0.5) * LOG2E
    stack = min(STACK, width // HEAD_DIM)
    core = lax.axis_index("dp") & 1
    turn = tile & 1

    def send(step, side, way):
        col = pl.multiple_of((core ^ side) * half + cols, HEAD_DIM)
        row = pl.multiple_of(step * step_rows, TILE)
        copy = pltpu.make_async_copy(
            buf.at[step & 1, side], out_ref.at[pl.ds(row, step_rows), pl.ds(col, width)], sem.at[step & 1, side]
        )
        copy.start() if way else copy.wait()

    @pl.when(tile >= 2)
    def _():
        for side in range(2):
            send(tile - 2, side, False)

    groups = []
    for part in range(step_rows // TILE):
        for side in range(2):
            for g in range(width // HEAD_DIM // stack):
                groups.append((part, side, g, *pairs[2 * side : 2 * side + 2]))

    def keys_of(part):
        return pl.ds(pl.multiple_of(tile * step_rows + part * TILE, TILE), span)

    def score_of(group):
        part, side, g, q_ref, kv_ref = group
        rows = jnp.concatenate(
            [
                q_ref[part * TILE : (part + 1) * TILE, h * HEAD_DIM : (h + 1) * HEAD_DIM]
                for h in range(g * stack, (g + 1) * stack)
            ],
            axis=0,
        )
        return lax.dot_general(
            rows, kv_ref[keys_of(part), :HEAD_DIM], (((1,), (1,)), ((), ())),
            preferred_element_type=jnp.float32,
        ).reshape(stack, TILE, span)

    def finish(group, weight, norm):
        part, side, g, q_ref, kv_ref = group
        mixed = jnp.dot(
            weight, kv_ref[keys_of(part), HEAD_DIM:], preferred_element_type=jnp.float32
        ).reshape(stack, TILE, HEAD_DIM)
        result = jnp.where(live[part][None], mixed / norm, 0.0).astype(jnp.bfloat16)
        for n in range(stack):
            h = g * stack + n
            buf[turn, side, part * TILE : (part + 1) * TILE, h * HEAD_DIM : (h + 1) * HEAD_DIM] = result[n]

    following, held = score_of(groups[0]), None
    for n, group in enumerate(groups):
        score = following
        following = score_of(groups[n + 1]) if n + 1 < len(groups) else None
        score = score * scale + bias[group[0]][None]
        peak = jnp.max(score, axis=2, keepdims=True)
        weight = jnp.exp2(score - peak)
        norm = jnp.sum(weight, axis=2, keepdims=True)
        if held is not None:
            finish(*held)
        held = group, weight.astype(jnp.bfloat16).reshape(stack * TILE, span), norm
    finish(*held)
    for side in range(2):
        send(tile, side, True)

    @pl.when(tile == last)
    def _():
        for side in range(2):
            send(tile - 1, side, False)
            send(tile, side, False)


def mix(plan, bias, own, far, out, full_width, col):
    (row_len, width), span = own[0].shape, bias.shape[1]
    operands = [plan, bias, *own, *far]
    step_rows = 2 * TILE if width <= 1024 else TILE
    rows = pl.BlockSpec((step_rows, width), lambda t, *_: (t, 0))
    whole = pl.BlockSpec(own[1].shape, lambda t, *_: (0, 0))
    specs = [pl.BlockSpec((step_rows, span), lambda t, *_: (t, 0)), rows, whole, rows, whole]
    aliases = {}
    if out is not None:
        aliases = {len(operands): 0}
        operands.append(out)
        specs.append(ANYWHERE)
    return pl.pallas_call(
        functools.partial(mix_kernel, cols=col, half=full_width // 2),
        grid_spec=pltpu.PrefetchScalarGridSpec(
            num_scalar_prefetch=1,
            grid=(row_len // step_rows,),
            in_specs=specs,
            out_specs=ANYWHERE,
            scratch_shapes=[
                pltpu.VMEM((2, 2, step_rows, width), jnp.bfloat16),
                pltpu.SemaphoreType.DMA((2, 2)),
            ],
        ),
        out_shape=jax.ShapeDtypeStruct((row_len, full_width), jnp.bfloat16),
        input_output_aliases=aliases,
        compiler_params=pltpu.CompilerParams(vmem_limit_bytes=32 << 20),
        cost_estimate=pl.CostEstimate(flops=0, transcendentals=0, bytes_accessed=SMALL),
        name="mix",
    )(*operands)


def after(value, *others):
    return lax.optimization_barrier((value, *others))[1:]


def eight_groups(queries, key_rows, value_rows, destination, token_count, doc_ids):
    ways = lax.axis_size("tensor")
    core = lax.axis_index("dp") & 1
    sentences, slot_len, q_width = queries.shape
    lanes = key_rows.shape[0]
    row_len = doc_ids.shape[1]
    half = q_width // 2
    kv_width = key_rows.shape[2] // ways
    full = 4 * (sentences // 4) * slot_len
    tiers = [(TIERS[-1], cap, cap, cap) for cap in TIERS] + [(full + 32,) * 4]
    def fetch_q(code, sources, into, sem, col, skip):
        own, near = sources
        width = into.shape[1]

        @pl.when(code < sentences)
        def _():
            base = pl.multiple_of((lax.axis_index("dp") & 1) * half + col, HEAD_DIM)
            pltpu.make_async_copy(own.at[code, :, pl.ds(base, width)], into, sem).start()

        @pl.when(code >= sentences)
        def _():
            pltpu.make_async_copy(
                near.at[code - sentences, :, pl.ds(col - skip, width)], into, sem
            ).start()

    def fetch_kv(code, sources, into, sem):
        own, near = sources
        from_level = (code & (sentences - 1)) // lanes
        lane = code & (lanes - 1)

        @pl.when(code < sentences)
        def _():
            pltpu.make_async_copy(own.at[from_level, 0, lane], into, sem).start()

        @pl.when(code >= sentences)
        def _():
            pltpu.make_async_copy(near.at[from_level, lane], into, sem).start()

    mine = jnp.stack([destination, token_count])
    table, load, number, near_first, kv = meet(
        mine, queries, key_rows, value_rows, lax.axis_size("dp"), ways, ROUNDS[0]
    )
    plan, tier, slots = make_plan(table, load, number, tiers)

    def with_caps(caps, widths, queries, near_first, plan, slots, doc_ids, kv):
        cols = [sum(widths[:n]) for n in range(len(widths))]
        rounds = len(widths)
        sent, arrived = [None] * rounds, [None] * rounds
        fresh = widths[0] != near_first.shape[2]
        skip = 0 if fresh else widths[0]

        def rest_of(core):
            start = pl.multiple_of(core * half + skip, HEAD_DIM)
            return slice(None), slice(None), pl.ds(start, half - skip)

        def others(core):
            return slice(None), 1

        def lend_rest(order, rows):
            return lend(
                rows, (sentences, slot_len, half - skip), rest_of, 4 if fresh else 1
            )

        def load(n, order):
            ready, base = (near_first, 0) if n == 0 and not fresh else (near, skip)
            sent[n] = post(
                order, slots, [queries, ready], functools.partial(fetch_q, col=cols[n], skip=base), caps,
                2 * sentences, slot_len, widths[n],
            )
            return after(sent[n][0], plan)[0]

        def depart(flows):
            far, beside, across = (swap(flows[f], 2 * f) for f in (3, 1, 2))
            return [flows[0], beside, across, far]

        if fresh:
            near = lend_rest(plan, queries)
        order = load(0, plan)
        arrived[0] = depart(sent[0])
        if rounds > 1:
            kept, order, kv, rows = lax.optimization_barrier((sent[0][0], plan, kv, queries))
            arrived[0][0] = kept
            near = lend_rest(order, rows)
        kv = lax.all_to_all(kv, "tensor", split_axis=0, concat_axis=0, tiled=True)
        if rounds > 1:
            order = load(1, order)
            order, *flows = after(arrived[0], order, *sent[1])
            arrived[1] = depart(flows)
        for n in range(2, min(rounds, 3)):
            order = load(n, order)
        waiting = list(range(3, rounds))
        docs, = after(order, doc_ids[0])

        live = jnp.arange(row_len, dtype=jnp.int32) < plan[INTO + 16 + 12]
        span = DOC_MAX + TILE
        padded = jnp.concatenate([jnp.full((DOC_MAX,), -1, jnp.int32), docs])
        tiles = row_len // TILE
        key_docs = jnp.stack([padded[t * TILE : t * TILE + span] for t in range(tiles)])
        col = jnp.arange(span, dtype=jnp.int32)[None, None, :]
        row = jnp.arange(TILE, dtype=jnp.int32)[None, :, None]
        allowed = (
            (col - DOC_MAX <= row)
            & (key_docs[:, None, :] == docs.reshape(tiles, TILE)[:, :, None])
            & live.reshape(tiles, TILE)[:, :, None]
        )
        bias = jnp.where(allowed, 0.0, NEG).astype(jnp.float32).reshape(row_len, span)

        order, = after(bias, order)
        steps = list(range(rounds))
        kv_turn = min(2, rounds)
        steps.insert(kv_turn, None)
        out, mixed = None, 0
        q_rows, kv_rows, kv_arrived = [None] * rounds, None, None

        def settle(step, order):
            nonlocal kv_rows
            if step is None:
                kv_away, kv_own = sort(order, kv_arrived, row_len, DOC_MAX)
                kv_rows = kv_own, lend(kv_away, kv_away.shape, None, 5)
                return after(kv_rows[1], plan)[0]
            q_away, q_own = sort(order, arrived[step], row_len, 0)
            q_far = lend(q_away, q_away.shape, None, 5 + sorted({*ROUNDS, half}).index(widths[step]) + 1)
            q_rows[step] = q_own, q_far
            return after(q_far, plan)[0]

        def load_kv(order):
            near_kv = lend(after(order, kv)[0], kv.shape[:1] + kv.shape[2:], others, 2)
            flows = post(
                order, slots, [kv, near_kv], fetch_kv, caps, 2 * sentences, slot_len, 2 * HEAD_DIM
            )
            return flows, after(flows[0], plan)[0]

        kv_sent = None
        for at in range(len(steps)):
            if at + 1 < len(steps):
                step = steps[at + 1]
                if step is None:
                    if kv_sent is None:
                        kv_sent, order = load_kv(order)
                    flows = kv_sent
                else:
                    flows = sent[step]
                here = kv_arrived if steps[at] is None else arrived[steps[at]]
                if step is None or arrived[step] is None:
                    order, *flows = after(here, order, *flows)
                    flows = depart(flows)
                    if step is None:
                        kv_arrived = flows
                    else:
                        arrived[step] = flows
            order = settle(steps[at], order)
            while kv_rows is not None and mixed < rounds and q_rows[mixed] is not None:
                q_own, q_far = q_rows[mixed]
                out = mix(
                    order, bias, (q_own, kv_rows[0]), (q_far, kv_rows[1]), out, q_width, cols[mixed]
                )
                order, = after(out, plan)
                mixed += 1
            if at and waiting:
                order = load(waiting.pop(0), order)
        return out

    return lax.switch(
        tier[0],
        [functools.partial(with_caps, caps, ROUNDS) for caps in tiers[:-1]]
        + [functools.partial(with_caps, tiers[-1], (half,))],
        queries, near_first, plan, slots, doc_ids, kv,
    )


def per_device(queries, key_rows, value_rows, destination, token_count, doc_ids):
    groups = lax.axis_size("dp")
    ways = lax.axis_size("tensor")
    me = lax.axis_index("dp")
    sentences = destination.shape[0]
    slot_len = queries.shape[1]
    row_len = doc_ids.shape[1]
    q_width = queries.shape[2]
    kv_width = key_rows.shape[2] // ways
    kv_local = kv_width // HEAD_DIM
    per_group = q_width // kv_width
    heads = min(CHUNK_HEADS, per_group)
    chunk_width = heads * HEAD_DIM

    if groups == 8:
        return eight_groups(queries, key_rows, value_rows, destination, token_count, doc_ids)

    table = lax.all_gather(jnp.stack([destination, token_count]), "dp", axis=0)

    def split(rows):
        return rows.reshape(rows.shape[0], slot_len, ways, kv_width)

    def own_heads(key_rows, value_rows):
        kv = jnp.concatenate([split(key_rows), split(value_rows)], axis=3)
        return lax.all_to_all(
            jnp.transpose(kv, (2, 0, 1, 3)), "tensor", split_axis=0, concat_axis=0, tiled=True
        ).reshape(sentences, slot_len, 2 * kv_width)

    dest = table[:, 0, :].reshape(-1)
    counts = table[:, 1, :].reshape(-1)
    source = jnp.repeat(jnp.arange(groups, dtype=jnp.int32), sentences)
    lane = jnp.tile(jnp.arange(sentences, dtype=jnp.int32), groups)

    count_of = lists_of((dest == me)[None], counts[None, None, :], sentences)[0]
    nth = jnp.arange(sentences, dtype=jnp.int32)
    ends = jnp.sum(jnp.where(nth[None, :] <= nth[:, None], count_of[None, :], 0), axis=1)
    place = jnp.arange(row_len, dtype=jnp.int32)
    passed = place[:, None] >= ends[None, :]
    which = jnp.sum(passed.astype(jnp.int32), axis=1)
    start = jnp.sum(jnp.where(passed, count_of[None, :], 0), axis=1)
    live = which < sentences
    spread = min(sentences, (TILE - 1 + LEAST - 1) // LEAST + 1)
    heads_of = place[::TILE]
    first = jnp.sum((heads_of[:, None] >= ends[None, :]).astype(jnp.int32), axis=1)
    first = jnp.minimum(first, sentences - spread)
    window = spread * slot_len
    relative = (which - jnp.repeat(first, TILE)) * slot_len + place - start
    pick = (
        live[:, None] & (relative[:, None] == jnp.arange(window, dtype=jnp.int32)[None, :])
    ).astype(jnp.bfloat16)
    span = DOC_MAX + TILE
    padded = jnp.concatenate([jnp.full((DOC_MAX,), -1, jnp.int32), doc_ids[0]])
    tiles = row_len // TILE
    key_docs = jnp.stack([padded[t * TILE : t * TILE + span] for t in range(tiles)])
    col = jnp.arange(span, dtype=jnp.int32)[None, None, :]
    row = jnp.arange(TILE, dtype=jnp.int32)[None, :, None]
    allowed = (
        (col - DOC_MAX <= row)
        & (key_docs[:, None, :] == doc_ids[0].reshape(tiles, TILE)[:, :, None])
        & live.reshape(tiles, TILE)[:, :, None]
    )
    bias = jnp.where(allowed, 0.0, NEG).astype(jnp.float32).reshape(row_len, span)

    chunks = q_width // chunk_width

    def attend_one(chunk, kv_packed, first, got, codes, out):
        return attend(
            codes, first, *kv_packed, pick, bias, *got, out, chunk, heads, chunk * heads // per_group, q_width
        )

    capacity = max(2, (2 * sentences + groups - 1) // groups)
    rank = lists_of(destination[None, :] == jnp.arange(groups, dtype=jnp.int32)[:, None], None, None)
    slot = jnp.arange(capacity, dtype=jnp.int32)
    at = rank[:, None, :] == slot[None, :, None]
    picked = jnp.sum(jnp.where(at, nth[None, None, :], 0), axis=2).reshape(-1)
    by_source = (dest == me).reshape(groups, sentences)
    rank_in = lists_of(by_source, None, None).reshape(-1)
    codes = lists_of(
        (dest == me)[None], (source * capacity + rank_in)[None, None, :], sentences
    )[0]

    def exchange(rows, col, width):
        sent = gather(picked, [rows], (col,), (0,), width)
        got = lax.all_to_all(sent, "dp", split_axis=0, concat_axis=0, tiled=True)
        return [got], (0,), (0,)

    got_kv = exchange(own_heads(key_rows, value_rows), 0, 2 * kv_width)
    got_q = [exchange(queries, n * chunk_width, chunk_width) for n in range(chunks)]
    kv_packed = pack(codes, first, pick, *got_kv, kv_local)
    out = None
    for n in range(chunks):
        out = attend_one(n, kv_packed, first, got_q[n], codes, out)
    return out


def solution(mesh):
    placed = (
        P("dp", None, "tensor"),
        P(("dp", "tensor"), None, None),
        P(("dp", "tensor"), None, None),
        P("dp"),
        P("dp"),
        P("dp", None),
    )
    return jax.shard_map(
        per_device, mesh=mesh, in_specs=placed, out_specs=P("dp", "tensor"), check_vma=False
    )
```

```python
import functools
import jax
import jax.numpy as jnp
from jax import lax
from jax.experimental import pallas as pl
from jax.experimental.pallas import tpu as pltpu
from jax.sharding import PartitionSpec as P

HEAD_DIM = 128
DOC_MAX = 256
LEAST = 16
TILE = 128
CHUNK_HEADS = 8
STACK = 4
SEND_TILE = 112
SPREAD = 12
SLOT = 32
SMALL = 1
UNROLLED = 8
VMEM = 56 << 20
ROUNDS = (512, 512, 512, 256, 256)
TIERS = (560, 704)
FAR = 1 << 20
CODE, START, COUNT, FIRST, INTO, TIER, PLAN = 0, 64, 128, 192, 256, 320, 336
NEG = -1e30
LOG2E = 1.4426950408889634
WHOLE = pl.BlockSpec(memory_space=pltpu.VMEM)
ANYWHERE = pl.BlockSpec(memory_space=pl.ANY)
FAR_OFF = pl.BlockSpec(memory_space=pltpu.HBM)
SCALARS = pl.BlockSpec(memory_space=pltpu.SMEM)


def fetch(code_ref, sources, cols, bases, buf, sem):
    def one(k, carry):
        code = code_ref[k]
        for i, (source, col) in enumerate(zip(sources, cols)):

            def start(i=i, source=source, col=col):
                pltpu.make_async_copy(
                    source.at[code - bases[i], :, pl.ds(col, buf.shape[2])], buf.at[k], sem
                ).start()

            if len(sources) == 1:
                start()
            else:
                inside = code >= bases[i]
                if i + 1 < len(sources):
                    inside = inside & (code < bases[i + 1])
                pl.when(inside)(start)
        return carry

    lax.fori_loop(0, buf.shape[0], one, 0, unroll=4 if buf.shape[0] % 4 == 0 else 1)


def gather_kernel(code_ref, *rest, cols, bases):
    *sources, out_ref, sem = rest
    fetch(code_ref, sources, cols, bases, out_ref, sem)
    pltpu.make_async_copy(out_ref, out_ref, sem).wait()


def gather(codes, sources, cols, bases, width):
    slot_len = sources[0].shape[1]
    shape = (codes.shape[0], slot_len, width)
    return pl.pallas_call(
        functools.partial(gather_kernel, cols=cols, bases=bases),
        grid_spec=pltpu.PrefetchScalarGridSpec(
            num_scalar_prefetch=1,
            grid=(1,),
            in_specs=[ANYWHERE] * len(sources),
            out_specs=pl.BlockSpec(shape, lambda i, *_: (0, 0, 0)),
            scratch_shapes=[pltpu.SemaphoreType.DMA],
        ),
        out_shape=jax.ShapeDtypeStruct(shape, sources[0].dtype),
        compiler_params=pltpu.CompilerParams(vmem_limit_bytes=16 << 20),
        cost_estimate=pl.CostEstimate(
            flops=0, transcendentals=0, bytes_accessed=4 * shape[0] * slot_len * width
        ),
        name="gather",
    )(codes, *sources)


def pack_kernel(code_ref, first_ref, pick_ref, *rest, cols, bases):
    *sources, k_ref, v_ref, buf, sem = rest
    kv_local, slot_len, window = k_ref.shape[0], buf.shape[1], pick_ref.shape[1]
    fetch(code_ref, sources, cols, bases, buf, sem)
    pltpu.make_async_copy(buf, buf, sem).wait()
    for ref in (k_ref, v_ref):
        ref[:, :DOC_MAX, :] = jnp.zeros((kv_local, DOC_MAX, HEAD_DIM), jnp.bfloat16)

    @pl.loop(0, pick_ref.shape[0] // TILE)
    def _(t):
        here = pl.multiple_of(t * TILE, TILE)
        rows = buf[pl.ds(first_ref[t], window // slot_len)].reshape(window, buf.shape[2])
        packed = jnp.dot(
            pick_ref[pl.ds(here, TILE), :], rows, preferred_element_type=jnp.float32
        ).astype(jnp.bfloat16)
        for n in range(2 * kv_local):
            ref = (k_ref, v_ref)[n // kv_local]
            ref[n % kv_local, pl.ds(DOC_MAX + here, TILE), :] = packed[
                :, n * HEAD_DIM : (n + 1) * HEAD_DIM
            ]


def pack(codes, first, pick, sources, cols, bases, kv_local):
    slot_len = sources[0].shape[1]
    shape = jax.ShapeDtypeStruct((kv_local, DOC_MAX + pick.shape[0], HEAD_DIM), jnp.bfloat16)
    return pl.pallas_call(
        functools.partial(pack_kernel, cols=cols, bases=bases),
        grid_spec=pltpu.PrefetchScalarGridSpec(
            num_scalar_prefetch=2,
            grid=(1,),
            in_specs=[WHOLE] + [ANYWHERE] * len(sources),
            out_specs=[WHOLE, WHOLE],
            scratch_shapes=[
                pltpu.VMEM((codes.shape[0], slot_len, 2 * kv_local * HEAD_DIM), jnp.bfloat16),
                pltpu.SemaphoreType.DMA,
            ],
        ),
        out_shape=[shape, shape],
        compiler_params=pltpu.CompilerParams(vmem_limit_bytes=16 << 20),
        name="pack",
    )(codes, first, pick, *sources)


def attend_kernel(code_ref, first_ref, k_ref, v_ref, pick_ref, bias_ref, *rest, cols, bases, heads):
    *sources, out_ref, q_buf, q_rows, sem = rest
    sources = sources[: len(cols)]
    tile = pl.program_id(0)
    slot_len, window = q_buf.shape[1], pick_ref.shape[1]
    span = bias_ref.shape[1]

    @pl.when(tile == 0)
    def _():
        fetch(code_ref, sources, cols, bases, q_buf, sem)
        pltpu.make_async_copy(q_buf, q_buf, sem).wait()

    here = pl.multiple_of(tile * TILE, TILE)
    pick = pick_ref[pl.ds(here, TILE), :]
    bias = bias_ref[pl.ds(here, TILE), :]
    live = jnp.max(bias, axis=1, keepdims=True) > -1.0
    keys = k_ref[pl.ds(here, span), :]
    values = v_ref[pl.ds(here, span), :]
    rows = q_buf[pl.ds(first_ref[tile], window // slot_len)].reshape(window, q_buf.shape[2])
    packed = jnp.dot(pick, rows, preferred_element_type=jnp.float32).astype(jnp.bfloat16)
    for h in range(heads):
        q_rows[h * TILE : (h + 1) * TILE, :] = packed[:, h * HEAD_DIM : (h + 1) * HEAD_DIM]
    scale = (HEAD_DIM**-0.5) * LOG2E
    stack = min(STACK, heads)
    for g in range(heads // stack):
        score = lax.dot_general(
            q_rows[g * stack * TILE : (g + 1) * stack * TILE, :],
            keys,
            (((1,), (1,)), ((), ())),
            preferred_element_type=jnp.float32,
        ).reshape(stack, TILE, span)
        score = score * scale + bias[None]
        peak = jnp.max(score, axis=2, keepdims=True)
        weight = jnp.exp2(score - peak)
        norm = jnp.sum(weight, axis=2, keepdims=True)
        mixed = jnp.dot(
            weight.astype(jnp.bfloat16).reshape(stack * TILE, span),
            values,
            preferred_element_type=jnp.float32,
        ).reshape(stack, TILE, HEAD_DIM)
        result = jnp.where(live[None], mixed / norm, 0.0).astype(jnp.bfloat16)
        for n in range(stack):
            h = g * stack + n
            out_ref[:, h * HEAD_DIM : (h + 1) * HEAD_DIM] = result[n]


def attend(codes, first, keys, values, pick, bias, sources, cols, bases, out, chunk, heads, kv_head, width):
    slot_len, (row_len, span) = sources[0].shape[1], bias.shape
    chunk_width = heads * HEAD_DIM
    one_head = pl.BlockSpec((None, DOC_MAX + row_len, HEAD_DIM), lambda t, *_: (kv_head, 0, 0))
    operands = [codes, first, keys, values, pick, bias, *sources]
    specs = [one_head, one_head, WHOLE, WHOLE] + [ANYWHERE] * len(sources)
    aliases = {}
    if out is not None:
        aliases = {len(operands): 0}
        operands.append(out)
        specs.append(ANYWHERE)
    return pl.pallas_call(
        functools.partial(attend_kernel, cols=cols, bases=bases, heads=heads),
        grid_spec=pltpu.PrefetchScalarGridSpec(
            num_scalar_prefetch=2,
            grid=(row_len // TILE,),
            in_specs=specs,
            out_specs=pl.BlockSpec((TILE, chunk_width), lambda t, *_: (t, chunk)),
            scratch_shapes=[
                pltpu.VMEM((codes.shape[0], slot_len, chunk_width), jnp.bfloat16),
                pltpu.VMEM((heads * TILE, HEAD_DIM), jnp.bfloat16),
                pltpu.SemaphoreType.DMA,
            ],
        ),
        out_shape=jax.ShapeDtypeStruct((row_len, width), jnp.bfloat16),
        input_output_aliases=aliases,
        compiler_params=pltpu.CompilerParams(vmem_limit_bytes=32 << 20),
        cost_estimate=pl.CostEstimate(
            flops=4 * row_len * span * chunk_width,
            transcendentals=row_len * span * heads,
            bytes_accessed=6 * row_len * chunk_width,
        ),
        name="attend",
    )(*operands)


def lists_of(masks, codes, slots):
    items = masks.shape[1]
    upto = jnp.arange(items)[:, None] <= jnp.arange(items)[None, :]
    rank = jnp.dot(
        masks.astype(jnp.bfloat16), upto.astype(jnp.bfloat16), preferred_element_type=jnp.float32
    ).astype(jnp.int32) - 1
    rank = jnp.where(masks, rank, -1)
    if codes is None:
        return rank
    at = rank[:, None, :] == jnp.arange(slots, dtype=jnp.int32)[None, :, None]
    return jnp.sum(jnp.where(at, codes, 0), axis=2)


def swap(rows, bit):
    pairs = [(i, i ^ bit) for i in range(lax.axis_size("dp"))]
    return lax.ppermute(rows, "dp", pairs)


MESH = pl.DeviceIdType.MESH


def meet_kernel(mine_ref, queries_ref, keys_ref, values_ref, table_ref, load_ref, count_ref, near_ref, *rest):
    kv_ref, send_sem, recv_sem = rest
    me, level = lax.axis_index("dp"), lax.axis_index("tensor")
    core = me & 1
    groups = table_ref.shape[0]
    half = queries_ref.shape[2] // 2
    barrier = pltpu.get_barrier_semaphore()
    for n in range(1, groups):
        pl.semaphore_signal(barrier, inc=1, device_id=(me ^ n, level), device_id_type=MESH)
    pl.semaphore_wait(barrier, groups - 1)
    copies = []
    for n in range(1, groups):
        copies.append(
            pltpu.make_async_remote_copy(
                mine_ref, table_ref.at[me], send_sem.at[n], recv_sem.at[n],
                device_id=(me ^ n, level), device_id_type=MESH,
            )
        )
    base = pl.multiple_of((core ^ 1) * half, HEAD_DIM)
    copies.append(
        pltpu.make_async_remote_copy(
            queries_ref.at[:, :, pl.ds(base, near_ref.shape[2])], near_ref, send_sem.at[0], recv_sem.at[0],
            device_id=(me ^ 1, level), device_id_type=MESH,
        )
    )
    for copy in copies:
        copy.start()
    table_ref[me] = mine_ref[...]
    for n in range(kv_ref.shape[0]):
        for part in range(2):
            head = pl.multiple_of((2 * n + (core ^ part)) * HEAD_DIM, HEAD_DIM)
            for kind, rows in enumerate((keys_ref, values_ref)):
                kv_ref[n, part, :, :, kind * HEAD_DIM : (kind + 1) * HEAD_DIM] = rows[:, :, pl.ds(head, HEAD_DIM)]
    for copy in copies[:-1]:
        copy.wait()
    dest, tokens = table_ref[:, 0, :], table_ref[:, 1, :]
    lane = lax.broadcasted_iota(jnp.int32, load_ref.shape, 1)
    load, count = jnp.zeros(load_ref.shape, jnp.int32), jnp.zeros(load_ref.shape, jnp.int32)
    for g in range(groups):
        load = jnp.where(lane == g, jnp.sum(jnp.where(dest == g, tokens, 0), axis=1, keepdims=True), load)
        count = jnp.where(lane == g, jnp.sum((dest == g).astype(jnp.int32), axis=1, keepdims=True), count)
    load_ref[...] = load
    count_ref[...] = count
    copies[-1].wait()


def meet(mine, queries, key_rows, value_rows, groups, ways, width):
    sentences, slot_len, _ = queries.shape
    bf16, i32 = jnp.bfloat16, jnp.int32
    small = jax.ShapeDtypeStruct((groups, groups), i32)
    kv = jax.ShapeDtypeStruct((ways, 2, key_rows.shape[0], slot_len, 2 * HEAD_DIM), bf16)
    return pl.pallas_call(
        meet_kernel,
        in_specs=[WHOLE, ANYWHERE, WHOLE, WHOLE],
        out_specs=[WHOLE, WHOLE, WHOLE, ANYWHERE, WHOLE],
        out_shape=[
            jax.ShapeDtypeStruct((groups, 2, sentences), i32), small, small,
            jax.ShapeDtypeStruct((sentences, slot_len, width), bf16),
            kv,
        ],
        scratch_shapes=[
            pltpu.SemaphoreType.DMA((groups,)),
            pltpu.SemaphoreType.DMA((groups,)),
        ],
        compiler_params=pltpu.CompilerParams(collective_id=0, has_side_effects=True),
        name="meet",
    )(mine, queries, key_rows, value_rows)


def plan_kernel(table_ref, load_ref, count_ref, plan_ref, tier_ref, slot_ref, begin_ref, shift_ref, key_ref, *, tiers):
    me = lax.axis_index("dp")
    chip, core = me >> 1, me & 1
    groups, _, sentences = table_ref.shape
    chips = groups // 2
    load = [[load_ref[2 * a, g] + load_ref[2 * a + 1, g] for g in range(groups)] for a in range(chips)]
    begin, totals = [[None] * groups for _ in range(chips)], [None] * groups
    for g in range(groups):
        total = jnp.int32(0)
        for a in range(chips):
            begin[a][g] = total
            total = total + load[a][g]
        totals[g] = total
    need = [jnp.int32(0)] * chips
    for a in range(chips):
        for b in range(chips):
            one = begin[a][2 * b] & (LEAST - 1)
            end = one + load[a][2 * b]
            two = end + ((begin[a][2 * b + 1] - end) & (LEAST - 1))
            need[a ^ b] = jnp.maximum(need[a ^ b], two + load[a][2 * b + 1])
            for g, first in ((2 * b, one), (2 * b + 1, two)):
                shift_ref[a * groups + g] = first
                begin_ref[a * groups + g] = begin[a][g]
    tier = jnp.int32(len(tiers) - 1)
    for n in reversed(range(len(tiers) - 1)):
        fits = functools.reduce(jnp.logical_and, [low <= cap for low, cap in zip(need, tiers[n])])
        tier = jnp.where(fits, n, tier)
    tier_ref[0] = tier
    passed = jnp.int32(0)
    for key in range(groups):
        group = key ^ (2 * chip)
        key_ref[key] = passed
        key_ref[groups + key] = shift_ref[chip * groups + group]
        for n in range(1, 16) if key % 2 else range(1):
            plan_ref[FIRST + 16 * (key // 2) + n] = passed
        passed = passed + count_ref[2 * chip, group] + count_ref[2 * chip + 1, group]
    for half in range(2):
        mine = sentences * (half ^ core)

        def place(n, carry, half=half, mine=mine):
            key = table_ref[2 * chip + half, 0, n] ^ (2 * chip)
            size = table_ref[2 * chip + half, 1, n]
            flow = key >> 1
            at, row = key_ref[key], key_ref[groups + key]
            plan_ref[CODE + at] = mine + n
            plan_ref[START + at] = flow * FAR + row
            plan_ref[COUNT + at] = size
            key_ref[key] = at + 1
            key_ref[groups + key] = row + size
            tile = ((row + SEND_TILE - 1) * 37450) >> 22
            plan_ref[FIRST + 16 * flow + jnp.where(tile * SEND_TILE < row + size, tile, 15)] = at
            return carry

        lax.fori_loop(0, sentences, place, 0, unroll=8)
    for order in range(2):
        group = 2 * chip + (core if order == 1 else 1 - core)
        for flow in range(chips):
            at = chip ^ flow
            plan_ref[INTO + 16 * order + flow] = begin_ref[at * groups + group]
            plan_ref[INTO + 16 * order + 4 + flow] = load_ref[2 * at, group] + load_ref[2 * at + 1, group]
            plan_ref[INTO + 16 * order + 8 + flow] = shift_ref[at * groups + group]
        plan_ref[INTO + 16 * order + 12] = begin_ref[(chips - 1) * groups + group] + (
            load_ref[2 * chips - 2, group] + load_ref[2 * chips - 1, group]
        )
    lane = lax.broadcasted_iota(jnp.int32, (1, HEAD_DIM), 1)
    token = lane % SLOT
    for r in range(slot_ref.shape[0]):
        start, size = jnp.zeros((1, HEAD_DIM), jnp.int32), jnp.zeros((1, HEAD_DIM), jnp.int32)
        for n in range(HEAD_DIM // SLOT):
            at = r * (HEAD_DIM // SLOT) + n
            start = jnp.where(lane // SLOT == n, plan_ref[START + at], start)
            size = jnp.where(lane // SLOT == n, plan_ref[COUNT + at], size)
        slot_ref[r : r + 1, :] = jnp.where(token < size, start + token, -1)


def make_plan(table, load, count, tiers):
    groups, _, sentences = table.shape
    cells = groups // 2 * groups
    return pl.pallas_call(
        functools.partial(plan_kernel, tiers=tiers),
        in_specs=[SCALARS] * 3,
        out_specs=[SCALARS, SCALARS, WHOLE],
        out_shape=[
            jax.ShapeDtypeStruct((PLAN,), jnp.int32),
            jax.ShapeDtypeStruct((1,), jnp.int32),
            jax.ShapeDtypeStruct((2 * sentences * SLOT // HEAD_DIM, HEAD_DIM), jnp.int32),
        ],
        scratch_shapes=[pltpu.SMEM((cells,), jnp.int32)] * 2 + [pltpu.SMEM((2 * groups,), jnp.int32)],
        name="plan",
    )(table, load, count)


def post_kernel(plan_ref, slot_ref, *rest, caps, fetch_one):
    sources, rest = rest[: -2 * len(caps) - 3], rest[-2 * len(caps) - 3 :]
    outs, (*tiles, buf, sem, out_sem) = rest[: len(caps)], rest[len(caps) :]
    slot_len, width = buf.shape[1:]

    def one(n, carry):
        fetch_one(plan_ref[CODE + n], sources, buf.at[n], sem)
        return carry

    lax.fori_loop(0, buf.shape[0], one, 0, unroll=4)
    pltpu.make_async_copy(buf, buf, sem).wait()
    per = HEAD_DIM // slot_len
    deep = SPREAD // per
    for flow, (cap, out) in enumerate(zip(caps, tiles)):

        def fill(tile, low, size, flow=flow, out=out):
            row = lax.broadcasted_iota(jnp.int32, (size, HEAD_DIM), 0) + (flow * FAR + low)
            first = jnp.minimum(plan_ref[FIRST + 16 * flow + tile] // per, slot_ref.shape[0] - deep)
            pick = jnp.concatenate(
                [
                    (row == slot_ref[pl.ds(first + n, 1), :]).astype(jnp.float32).astype(jnp.bfloat16)
                    for n in range(deep)
                ],
                axis=1,
            )
            rows = buf[pl.ds(first * per, SPREAD)].reshape(SPREAD * slot_len, width)
            out[pl.ds(low, size), :] = jnp.dot(pick, rows, preferred_element_type=jnp.float32).astype(
                jnp.bfloat16
            )

        whole = cap // SEND_TILE
        if whole <= UNROLLED:
            for tile in range(whole):
                fill(tile, tile * SEND_TILE, SEND_TILE)
        else:

            @pl.loop(0, whole)
            def _(tile, fill=fill):
                fill(tile, pl.multiple_of(tile * SEND_TILE, LEAST), SEND_TILE)

        left = cap % SEND_TILE
        if left:
            fill(whole, cap - left, left)
        pltpu.make_async_copy(out, outs[flow], out_sem.at[flow]).start()
    for flow, out in enumerate(tiles):
        pltpu.make_async_copy(out, outs[flow], out_sem.at[flow]).wait()


def post(plan, slots, sources, fetch_one, caps, count, slot_len, width):
    shapes = [jax.ShapeDtypeStruct((cap, width), jnp.bfloat16) for cap in caps]
    return pl.pallas_call(
        functools.partial(post_kernel, caps=caps, fetch_one=fetch_one),
        grid_spec=pltpu.PrefetchScalarGridSpec(
            num_scalar_prefetch=1,
            grid=(1,),
            in_specs=[WHOLE] + [FAR_OFF] * len(sources),
            out_specs=[FAR_OFF] * len(caps),
            scratch_shapes=[pltpu.VMEM(shape.shape, shape.dtype) for shape in shapes] + [
                pltpu.VMEM((count, slot_len, width), jnp.bfloat16),
                pltpu.SemaphoreType.DMA,
                pltpu.SemaphoreType.DMA((len(caps),)),
            ],
        ),
        out_shape=shapes,
        compiler_params=pltpu.CompilerParams(vmem_limit_bytes=VMEM),
        cost_estimate=pl.CostEstimate(
            flops=0,
            transcendentals=0,
            bytes_accessed=SMALL,
        ),
        name="post",
    )(plan, slots, *sources)


def lend_kernel(rows_ref, out_ref, send_sem, recv_sem, *, region):
    me, level = lax.axis_index("dp"), lax.axis_index("tensor")
    barrier = pltpu.get_barrier_semaphore()
    pl.semaphore_signal(barrier, inc=1, device_id=(me ^ 1, level), device_id_type=MESH)
    pl.semaphore_wait(barrier, 1)
    copy = pltpu.make_async_remote_copy(
        rows_ref.at[region((me & 1) ^ 1)] if region else rows_ref, out_ref, send_sem, recv_sem,
        device_id=(me ^ 1, level), device_id_type=MESH,
    )
    copy.start()
    copy.wait()


def lend(rows, shape, region, number):
    return pl.pallas_call(
        functools.partial(lend_kernel, region=region),
        in_specs=[ANYWHERE],
        out_specs=ANYWHERE,
        out_shape=jax.ShapeDtypeStruct(shape, rows.dtype),
        scratch_shapes=[pltpu.SemaphoreType.DMA] * 2,
        compiler_params=pltpu.CompilerParams(
            collective_id=number, has_side_effects=True, vmem_limit_bytes=4 << 20
        ),
        cost_estimate=pl.CostEstimate(flops=0, transcendentals=0, bytes_accessed=SMALL),
        name="lend",
    )(rows)


def sort_kernel(plan_ref, *rest, caps, lead):
    flows, (away, own_ref, buf, sem) = rest[: len(caps)], rest[len(caps) :]
    row_len, width = own_ref.shape[0] - lead, own_ref.shape[1]
    for f, (cap, flow) in enumerate(zip(caps, flows)):
        pltpu.make_async_copy(flow, buf.at[f, pl.ds(TILE, cap)], sem.at[f]).start()
    for f, cap in enumerate(caps):
        for low in (0, TILE + cap):
            buf[f, low : low + TILE, :] = jnp.zeros((TILE, width), jnp.bfloat16)
    if lead:
        for out in (away, own_ref):
            out[:lead, :] = jnp.zeros((lead, width), jnp.bfloat16)
    for f, (cap, flow) in enumerate(zip(caps, flows)):
        pltpu.make_async_copy(flow, buf.at[f, pl.ds(TILE, cap)], sem.at[f]).wait()
    row = lax.broadcasted_iota(jnp.int32, (TILE, HEAD_DIM), 0)

    def fill(order, out):
        @pl.loop(0, row_len // TILE)
        def _(t):
            here = pl.multiple_of(t * TILE, TILE)
            total = None
            for f, cap in enumerate(caps):
                begin = plan_ref[INTO + 16 * order + f] - here
                size = plan_ref[INTO + 16 * order + 4 + f]
                low = plan_ref[INTO + 16 * order + 8 + f] - begin + TILE
                low = pl.multiple_of(jnp.clip(low, 0, TILE + cap), LEAST)
                mask = ((row >= begin) & (row < begin + size)).astype(jnp.float32).astype(jnp.bfloat16)
                mask = jnp.concatenate([mask] * (width // HEAD_DIM), axis=1)
                part = buf[f, pl.ds(low, TILE), :] * mask
                total = part if total is None else total + part
            out[pl.ds(lead + here, TILE), :] = total

    fill(0, away)
    fill(1, own_ref)


def sort(plan, flows, row_len, lead):
    caps = tuple(flow.shape[0] for flow in flows)
    width = flows[0].shape[1]
    shape = jax.ShapeDtypeStruct((lead + row_len, width), jnp.bfloat16)
    return pl.pallas_call(
        functools.partial(sort_kernel, caps=caps, lead=lead),
        in_specs=[SCALARS] + [ANYWHERE] * len(flows),
        out_specs=[WHOLE, WHOLE],
        out_shape=[shape, shape],
        scratch_shapes=[
            pltpu.VMEM((len(caps), max(caps) + 2 * TILE, width), jnp.bfloat16),
            pltpu.SemaphoreType.DMA((len(caps),)),
        ],
        compiler_params=pltpu.CompilerParams(
            vmem_limit_bytes=VMEM if width > 1024 else 24 << 20,
        ),
        cost_estimate=pl.CostEstimate(flops=0, transcendentals=0, bytes_accessed=SMALL),
        name="sort",
    )(plan, *flows)


def mix_kernel(plan_ref, bias_ref, *rest, cols, half):
    pairs, (*_, out_ref, buf, sem) = rest[:4], rest[4:]
    tile, last = pl.program_id(0), pl.num_programs(0) - 1
    span = bias_ref.shape[1]
    width = pairs[0].shape[1]
    step_rows = buf.shape[2]
    bias = [bias_ref[low : low + TILE, :] for low in range(0, step_rows, TILE)]
    live = [jnp.max(one, axis=1, keepdims=True) > -1.0 for one in bias]
    scale = (HEAD_DIM**-0.5) * LOG2E
    stack = min(STACK, width // HEAD_DIM)
    core = lax.axis_index("dp") & 1
    turn = tile & 1

    def send(step, side, way):
        col = pl.multiple_of((core ^ side) * half + cols, HEAD_DIM)
        row = pl.multiple_of(step * step_rows, TILE)
        copy = pltpu.make_async_copy(
            buf.at[step & 1, side], out_ref.at[pl.ds(row, step_rows), pl.ds(col, width)], sem.at[step & 1, side]
        )
        copy.start() if way else copy.wait()

    @pl.when(tile >= 2)
    def _():
        for side in range(2):
            send(tile - 2, side, False)

    groups = []
    for part in range(step_rows // TILE):
        for side in range(2):
            for g in range(width // HEAD_DIM // stack):
                groups.append((part, side, g, *pairs[2 * side : 2 * side + 2]))

    def keys_of(part):
        return pl.ds(pl.multiple_of(tile * step_rows + part * TILE, TILE), span)

    def score_of(group):
        part, side, g, q_ref, kv_ref = group
        rows = jnp.concatenate(
            [
                q_ref[part * TILE : (part + 1) * TILE, h * HEAD_DIM : (h + 1) * HEAD_DIM]
                for h in range(g * stack, (g + 1) * stack)
            ],
            axis=0,
        )
        return lax.dot_general(
            rows, kv_ref[keys_of(part), :HEAD_DIM], (((1,), (1,)), ((), ())),
            preferred_element_type=jnp.float32,
        ).reshape(stack, TILE, span)

    def finish(group, weight, norm):
        part, side, g, q_ref, kv_ref = group
        mixed = jnp.dot(
            weight, kv_ref[keys_of(part), HEAD_DIM:], preferred_element_type=jnp.float32
        ).reshape(stack, TILE, HEAD_DIM)
        result = jnp.where(live[part][None], mixed / norm, 0.0).astype(jnp.bfloat16)
        for n in range(stack):
            h = g * stack + n
            buf[turn, side, part * TILE : (part + 1) * TILE, h * HEAD_DIM : (h + 1) * HEAD_DIM] = result[n]

    following, held = score_of(groups[0]), None
    for n, group in enumerate(groups):
        score = following
        following = score_of(groups[n + 1]) if n + 1 < len(groups) else None
        score = score * scale + bias[group[0]][None]
        peak = jnp.max(score, axis=2, keepdims=True)
        weight = jnp.exp2(score - peak)
        norm = jnp.sum(weight, axis=2, keepdims=True)
        if held is not None:
            finish(*held)
        held = group, weight.astype(jnp.bfloat16).reshape(stack * TILE, span), norm
    finish(*held)
    for side in range(2):
        send(tile, side, True)

    @pl.when(tile == last)
    def _():
        for side in range(2):
            send(tile - 1, side, False)
            send(tile, side, False)


def mix(plan, bias, own, far, out, full_width, col):
    (row_len, width), span = own[0].shape, bias.shape[1]
    operands = [plan, bias, *own, *far]
    step_rows = 2 * TILE if width <= 1024 else TILE
    rows = pl.BlockSpec((step_rows, width), lambda t, *_: (t, 0))
    whole = pl.BlockSpec(own[1].shape, lambda t, *_: (0, 0))
    specs = [pl.BlockSpec((step_rows, span), lambda t, *_: (t, 0)), rows, whole, rows, whole]
    aliases = {}
    if out is not None:
        aliases = {len(operands): 0}
        operands.append(out)
        specs.append(ANYWHERE)
    return pl.pallas_call(
        functools.partial(mix_kernel, cols=col, half=full_width // 2),
        grid_spec=pltpu.PrefetchScalarGridSpec(
            num_scalar_prefetch=1,
            grid=(row_len // step_rows,),
            in_specs=specs,
            out_specs=ANYWHERE,
            scratch_shapes=[
                pltpu.VMEM((2, 2, step_rows, width), jnp.bfloat16),
                pltpu.SemaphoreType.DMA((2, 2)),
            ],
        ),
        out_shape=jax.ShapeDtypeStruct((row_len, full_width), jnp.bfloat16),
        input_output_aliases=aliases,
        compiler_params=pltpu.CompilerParams(vmem_limit_bytes=32 << 20),
        cost_estimate=pl.CostEstimate(flops=0, transcendentals=0, bytes_accessed=SMALL),
        name="mix",
    )(*operands)


def after(value, *others):
    return lax.optimization_barrier((value, *others))[1:]


def eight_groups(queries, key_rows, value_rows, destination, token_count, doc_ids):
    ways = lax.axis_size("tensor")
    core = lax.axis_index("dp") & 1
    sentences, slot_len, q_width = queries.shape
    lanes = key_rows.shape[0]
    row_len = doc_ids.shape[1]
    half = q_width // 2
    kv_width = key_rows.shape[2] // ways
    full = 4 * (sentences // 4) * slot_len
    tiers = [(TIERS[-1], cap, cap, cap) for cap in TIERS] + [(full + 32,) * 4]
    def fetch_q(code, sources, into, sem, col, skip):
        own, near = sources
        width = into.shape[1]

        @pl.when(code < sentences)
        def _():
            base = pl.multiple_of((lax.axis_index("dp") & 1) * half + col, HEAD_DIM)
            pltpu.make_async_copy(own.at[code, :, pl.ds(base, width)], into, sem).start()

        @pl.when(code >= sentences)
        def _():
            pltpu.make_async_copy(
                near.at[code - sentences, :, pl.ds(col - skip, width)], into, sem
            ).start()

    def fetch_kv(code, sources, into, sem):
        own, near = sources
        from_level = (code & (sentences - 1)) // lanes
        lane = code & (lanes - 1)

        @pl.when(code < sentences)
        def _():
            pltpu.make_async_copy(own.at[from_level, 0, lane], into, sem).start()

        @pl.when(code >= sentences)
        def _():
            pltpu.make_async_copy(near.at[from_level, lane], into, sem).start()

    mine = jnp.stack([destination, token_count])
    table, load, number, near_first, kv = meet(
        mine, queries, key_rows, value_rows, lax.axis_size("dp"), ways, ROUNDS[0]
    )
    plan, tier, slots = make_plan(table, load, number, tiers)

    def with_caps(caps, widths, queries, near_first, plan, slots, doc_ids, kv):
        cols = [sum(widths[:n]) for n in range(len(widths))]
        rounds = len(widths)
        sent, arrived = [None] * rounds, [None] * rounds
        fresh = widths[0] != near_first.shape[2]
        skip = 0 if fresh else widths[0]

        def rest_of(core):
            start = pl.multiple_of(core * half + skip, HEAD_DIM)
            return slice(None), slice(None), pl.ds(start, half - skip)

        def others(core):
            return slice(None), 1

        def lend_rest(order, rows):
            return lend(
                rows, (sentences, slot_len, half - skip), rest_of, 4 if fresh else 1
            )

        def load(n, order):
            ready, base = (near_first, 0) if n == 0 and not fresh else (near, skip)
            sent[n] = post(
                order, slots, [queries, ready], functools.partial(fetch_q, col=cols[n], skip=base), caps,
                2 * sentences, slot_len, widths[n],
            )
            return after(sent[n][0], plan)[0]

        def depart(flows):
            far, beside, across = (swap(flows[f], 2 * f) for f in (3, 1, 2))
            return [flows[0], beside, across, far]

        if fresh:
            near = lend_rest(plan, queries)
        order = load(0, plan)
        arrived[0] = depart(sent[0])
        if rounds > 1:
            kept, order, kv, rows = lax.optimization_barrier((sent[0][0], plan, kv, queries))
            arrived[0][0] = kept
            near = lend_rest(order, rows)
        kv = lax.all_to_all(kv, "tensor", split_axis=0, concat_axis=0, tiled=True)
        if rounds > 1:
            order = load(1, order)
            order, *flows = after(arrived[0], order, *sent[1])
            arrived[1] = depart(flows)
        for n in range(2, min(rounds, 3)):
            order = load(n, order)
        waiting = list(range(3, rounds))
        docs, = after(order, doc_ids[0])

        live = jnp.arange(row_len, dtype=jnp.int32) < plan[INTO + 16 + 12]
        span = DOC_MAX + TILE
        padded = jnp.concatenate([jnp.full((DOC_MAX,), -1, jnp.int32), docs])
        tiles = row_len // TILE
        key_docs = jnp.stack([padded[t * TILE : t * TILE + span] for t in range(tiles)])
        col = jnp.arange(span, dtype=jnp.int32)[None, None, :]
        row = jnp.arange(TILE, dtype=jnp.int32)[None, :, None]
        allowed = (
            (col - DOC_MAX <= row)
            & (key_docs[:, None, :] == docs.reshape(tiles, TILE)[:, :, None])
            & live.reshape(tiles, TILE)[:, :, None]
        )
        bias = jnp.where(allowed, 0.0, NEG).astype(jnp.float32).reshape(row_len, span)

        order, = after(bias, order)
        steps = list(range(rounds))
        kv_turn = min(2, rounds)
        steps.insert(kv_turn, None)
        out, mixed = None, 0
        q_rows, kv_rows, kv_arrived = [None] * rounds, None, None

        def settle(step, order):
            nonlocal kv_rows
            if step is None:
                kv_away, kv_own = sort(order, kv_arrived, row_len, DOC_MAX)
                kv_rows = kv_own, lend(kv_away, kv_away.shape, None, 5)
                return after(kv_rows[1], plan)[0]
            q_away, q_own = sort(order, arrived[step], row_len, 0)
            q_far = lend(q_away, q_away.shape, None, 5 + sorted({*ROUNDS, half}).index(widths[step]) + 1)
            q_rows[step] = q_own, q_far
            return after(q_far, plan)[0]

        def load_kv(order):
            near_kv = lend(after(order, kv)[0], kv.shape[:1] + kv.shape[2:], others, 2)
            flows = post(
                order, slots, [kv, near_kv], fetch_kv, caps, 2 * sentences, slot_len, 2 * HEAD_DIM
            )
            return flows, after(flows[0], plan)[0]

        kv_sent = None
        for at in range(len(steps)):
            if at + 1 < len(steps):
                step = steps[at + 1]
                if step is None:
                    if kv_sent is None:
                        kv_sent, order = load_kv(order)
                    flows = kv_sent
                else:
                    flows = sent[step]
                here = kv_arrived if steps[at] is None else arrived[steps[at]]
                if step is None or arrived[step] is None:
                    order, *flows = after(here, order, *flows)
                    flows = depart(flows)
                    if step is None:
                        kv_arrived = flows
                    else:
                        arrived[step] = flows
            order = settle(steps[at], order)
            while kv_rows is not None and mixed < rounds and q_rows[mixed] is not None:
                q_own, q_far = q_rows[mixed]
                out = mix(
                    order, bias, (q_own, kv_rows[0]), (q_far, kv_rows[1]), out, q_width, cols[mixed]
                )
                order, = after(out, plan)
                mixed += 1
            if at and waiting:
                order = load(waiting.pop(0), order)
        return out

    return lax.switch(
        tier[0],
        [functools.partial(with_caps, caps, ROUNDS) for caps in tiers[:-1]]
        + [functools.partial(with_caps, tiers[-1], (half,))],
        queries, near_first, plan, slots, doc_ids, kv,
    )


def per_device(queries, key_rows, value_rows, destination, token_count, doc_ids):
    groups = lax.axis_size("dp")
    ways = lax.axis_size("tensor")
    me = lax.axis_index("dp")
    sentences = destination.shape[0]
    slot_len = queries.shape[1]
    row_len = doc_ids.shape[1]
    q_width = queries.shape[2]
    kv_width = key_rows.shape[2] // ways
    kv_local = kv_width // HEAD_DIM
    per_group = q_width // kv_width
    heads = min(CHUNK_HEADS, per_group)
    chunk_width = heads * HEAD_DIM

    if groups == 8:
        return eight_groups(queries, key_rows, value_rows, destination, token_count, doc_ids)

    table = lax.all_gather(jnp.stack([destination, token_count]), "dp", axis=0)

    def split(rows):
        return rows.reshape(rows.shape[0], slot_len, ways, kv_width)

    def own_heads(key_rows, value_rows):
        kv = jnp.concatenate([split(key_rows), split(value_rows)], axis=3)
        return lax.all_to_all(
            jnp.transpose(kv, (2, 0, 1, 3)), "tensor", split_axis=0, concat_axis=0, tiled=True
        ).reshape(sentences, slot_len, 2 * kv_width)

    dest = table[:, 0, :].reshape(-1)
    counts = table[:, 1, :].reshape(-1)
    source = jnp.repeat(jnp.arange(groups, dtype=jnp.int32), sentences)
    lane = jnp.tile(jnp.arange(sentences, dtype=jnp.int32), groups)

    count_of = lists_of((dest == me)[None], counts[None, None, :], sentences)[0]
    nth = jnp.arange(sentences, dtype=jnp.int32)
    ends = jnp.sum(jnp.where(nth[None, :] <= nth[:, None], count_of[None, :], 0), axis=1)
    place = jnp.arange(row_len, dtype=jnp.int32)
    passed = place[:, None] >= ends[None, :]
    which = jnp.sum(passed.astype(jnp.int32), axis=1)
    start = jnp.sum(jnp.where(passed, count_of[None, :], 0), axis=1)
    live = which < sentences
    spread = min(sentences, (TILE - 1 + LEAST - 1) // LEAST + 1)
    heads_of = place[::TILE]
    first = jnp.sum((heads_of[:, None] >= ends[None, :]).astype(jnp.int32), axis=1)
    first = jnp.minimum(first, sentences - spread)
    window = spread * slot_len
    relative = (which - jnp.repeat(first, TILE)) * slot_len + place - start
    pick = (
        live[:, None] & (relative[:, None] == jnp.arange(window, dtype=jnp.int32)[None, :])
    ).astype(jnp.bfloat16)
    span = DOC_MAX + TILE
    padded = jnp.concatenate([jnp.full((DOC_MAX,), -1, jnp.int32), doc_ids[0]])
    tiles = row_len // TILE
    key_docs = jnp.stack([padded[t * TILE : t * TILE + span] for t in range(tiles)])
    col = jnp.arange(span, dtype=jnp.int32)[None, None, :]
    row = jnp.arange(TILE, dtype=jnp.int32)[None, :, None]
    allowed = (
        (col - DOC_MAX <= row)
        & (key_docs[:, None, :] == doc_ids[0].reshape(tiles, TILE)[:, :, None])
        & live.reshape(tiles, TILE)[:, :, None]
    )
    bias = jnp.where(allowed, 0.0, NEG).astype(jnp.float32).reshape(row_len, span)

    chunks = q_width // chunk_width

    def attend_one(chunk, kv_packed, first, got, codes, out):
        return attend(
            codes, first, *kv_packed, pick, bias, *got, out, chunk, heads, chunk * heads // per_group, q_width
        )

    capacity = max(2, (2 * sentences + groups - 1) // groups)
    rank = lists_of(destination[None, :] == jnp.arange(groups, dtype=jnp.int32)[:, None], None, None)
    slot = jnp.arange(capacity, dtype=jnp.int32)
    at = rank[:, None, :] == slot[None, :, None]
    picked = jnp.sum(jnp.where(at, nth[None, None, :], 0), axis=2).reshape(-1)
    by_source = (dest == me).reshape(groups, sentences)
    rank_in = lists_of(by_source, None, None).reshape(-1)
    codes = lists_of(
        (dest == me)[None], (source * capacity + rank_in)[None, None, :], sentences
    )[0]

    def exchange(rows, col, width):
        sent = gather(picked, [rows], (col,), (0,), width)
        got = lax.all_to_all(sent, "dp", split_axis=0, concat_axis=0, tiled=True)
        return [got], (0,), (0,)

    got_kv = exchange(own_heads(key_rows, value_rows), 0, 2 * kv_width)
    got_q = [exchange(queries, n * chunk_width, chunk_width) for n in range(chunks)]
    kv_packed = pack(codes, first, pick, *got_kv, kv_local)
    out = None
    for n in range(chunks):
        out = attend_one(n, kv_packed, first, got_q[n], codes, out)
    return out


def solution(mesh):
    placed = (
        P("dp", None, "tensor"),
        P(("dp", "tensor"), None, None),
        P(("dp", "tensor"), None, None),
        P("dp"),
        P("dp"),
        P("dp", None),
    )
    return jax.shard_map(
        per_device, mesh=mesh, in_specs=placed, out_specs=P("dp", "tensor"), check_vma=False
    )
```

```python
import functools
import jax
import jax.numpy as jnp
from jax import lax
from jax.experimental import pallas as pl
from jax.experimental.pallas import tpu as pltpu
from jax.sharding import PartitionSpec as P

HEAD_DIM = 128
DOC_MAX = 256
LEAST = 16
TILE = 128
CHUNK_HEADS = 8
STACK = 4
SEND_TILE = 112
SPREAD = 12
SLOT = 32
SMALL = 1
UNROLLED = 8
VMEM = 56 << 20
ROUNDS = (256, 512, 512, 512, 256)
TIERS = (560, 704)
FAR = 1 << 20
CODE, START, COUNT, FIRST, INTO, TIER, PLAN = 0, 64, 128, 192, 256, 320, 336
NEG = -1e30
LOG2E = 1.4426950408889634
WHOLE = pl.BlockSpec(memory_space=pltpu.VMEM)
ANYWHERE = pl.BlockSpec(memory_space=pl.ANY)
FAR_OFF = pl.BlockSpec(memory_space=pltpu.HBM)
SCALARS = pl.BlockSpec(memory_space=pltpu.SMEM)


def fetch(code_ref, sources, cols, bases, buf, sem):
    def one(k, carry):
        code = code_ref[k]
        for i, (source, col) in enumerate(zip(sources, cols)):

            def start(i=i, source=source, col=col):
                pltpu.make_async_copy(
                    source.at[code - bases[i], :, pl.ds(col, buf.shape[2])], buf.at[k], sem
                ).start()

            if len(sources) == 1:
                start()
            else:
                inside = code >= bases[i]
                if i + 1 < len(sources):
                    inside = inside & (code < bases[i + 1])
                pl.when(inside)(start)
        return carry

    lax.fori_loop(0, buf.shape[0], one, 0, unroll=4 if buf.shape[0] % 4 == 0 else 1)


def gather_kernel(code_ref, *rest, cols, bases):
    *sources, out_ref, sem = rest
    fetch(code_ref, sources, cols, bases, out_ref, sem)
    pltpu.make_async_copy(out_ref, out_ref, sem).wait()


def gather(codes, sources, cols, bases, width):
    slot_len = sources[0].shape[1]
    shape = (codes.shape[0], slot_len, width)
    return pl.pallas_call(
        functools.partial(gather_kernel, cols=cols, bases=bases),
        grid_spec=pltpu.PrefetchScalarGridSpec(
            num_scalar_prefetch=1,
            grid=(1,),
            in_specs=[ANYWHERE] * len(sources),
            out_specs=pl.BlockSpec(shape, lambda i, *_: (0, 0, 0)),
            scratch_shapes=[pltpu.SemaphoreType.DMA],
        ),
        out_shape=jax.ShapeDtypeStruct(shape, sources[0].dtype),
        compiler_params=pltpu.CompilerParams(vmem_limit_bytes=16 << 20),
        cost_estimate=pl.CostEstimate(
            flops=0, transcendentals=0, bytes_accessed=4 * shape[0] * slot_len * width
        ),
        name="gather",
    )(codes, *sources)


def pack_kernel(code_ref, first_ref, pick_ref, *rest, cols, bases):
    *sources, k_ref, v_ref, buf, sem = rest
    kv_local, slot_len, window = k_ref.shape[0], buf.shape[1], pick_ref.shape[1]
    fetch(code_ref, sources, cols, bases, buf, sem)
    pltpu.make_async_copy(buf, buf, sem).wait()
    for ref in (k_ref, v_ref):
        ref[:, :DOC_MAX, :] = jnp.zeros((kv_local, DOC_MAX, HEAD_DIM), jnp.bfloat16)

    @pl.loop(0, pick_ref.shape[0] // TILE)
    def _(t):
        here = pl.multiple_of(t * TILE, TILE)
        rows = buf[pl.ds(first_ref[t], window // slot_len)].reshape(window, buf.shape[2])
        packed = jnp.dot(
            pick_ref[pl.ds(here, TILE), :], rows, preferred_element_type=jnp.float32
        ).astype(jnp.bfloat16)
        for n in range(2 * kv_local):
            ref = (k_ref, v_ref)[n // kv_local]
            ref[n % kv_local, pl.ds(DOC_MAX + here, TILE), :] = packed[
                :, n * HEAD_DIM : (n + 1) * HEAD_DIM
            ]


def pack(codes, first, pick, sources, cols, bases, kv_local):
    slot_len = sources[0].shape[1]
    shape = jax.ShapeDtypeStruct((kv_local, DOC_MAX + pick.shape[0], HEAD_DIM), jnp.bfloat16)
    return pl.pallas_call(
        functools.partial(pack_kernel, cols=cols, bases=bases),
        grid_spec=pltpu.PrefetchScalarGridSpec(
            num_scalar_prefetch=2,
            grid=(1,),
            in_specs=[WHOLE] + [ANYWHERE] * len(sources),
            out_specs=[WHOLE, WHOLE],
            scratch_shapes=[
                pltpu.VMEM((codes.shape[0], slot_len, 2 * kv_local * HEAD_DIM), jnp.bfloat16),
                pltpu.SemaphoreType.DMA,
            ],
        ),
        out_shape=[shape, shape],
        compiler_params=pltpu.CompilerParams(vmem_limit_bytes=16 << 20),
        name="pack",
    )(codes, first, pick, *sources)


def attend_kernel(code_ref, first_ref, k_ref, v_ref, pick_ref, bias_ref, *rest, cols, bases, heads):
    *sources, out_ref, q_buf, q_rows, sem = rest
    sources = sources[: len(cols)]
    tile = pl.program_id(0)
    slot_len, window = q_buf.shape[1], pick_ref.shape[1]
    span = bias_ref.shape[1]

    @pl.when(tile == 0)
    def _():
        fetch(code_ref, sources, cols, bases, q_buf, sem)
        pltpu.make_async_copy(q_buf, q_buf, sem).wait()

    here = pl.multiple_of(tile * TILE, TILE)
    pick = pick_ref[pl.ds(here, TILE), :]
    bias = bias_ref[pl.ds(here, TILE), :]
    live = jnp.max(bias, axis=1, keepdims=True) > -1.0
    keys = k_ref[pl.ds(here, span), :]
    values = v_ref[pl.ds(here, span), :]
    rows = q_buf[pl.ds(first_ref[tile], window // slot_len)].reshape(window, q_buf.shape[2])
    packed = jnp.dot(pick, rows, preferred_element_type=jnp.float32).astype(jnp.bfloat16)
    for h in range(heads):
        q_rows[h * TILE : (h + 1) * TILE, :] = packed[:, h * HEAD_DIM : (h + 1) * HEAD_DIM]
    scale = (HEAD_DIM**-0.5) * LOG2E
    stack = min(STACK, heads)
    for g in range(heads // stack):
        score = lax.dot_general(
            q_rows[g * stack * TILE : (g + 1) * stack * TILE, :],
            keys,
            (((1,), (1,)), ((), ())),
            preferred_element_type=jnp.float32,
        ).reshape(stack, TILE, span)
        score = score * scale + bias[None]
        peak = jnp.max(score, axis=2, keepdims=True)
        weight = jnp.exp2(score - peak)
        norm = jnp.sum(weight, axis=2, keepdims=True)
        mixed = jnp.dot(
            weight.astype(jnp.bfloat16).reshape(stack * TILE, span),
            values,
            preferred_element_type=jnp.float32,
        ).reshape(stack, TILE, HEAD_DIM)
        result = jnp.where(live[None], mixed / norm, 0.0).astype(jnp.bfloat16)
        for n in range(stack):
            h = g * stack + n
            out_ref[:, h * HEAD_DIM : (h + 1) * HEAD_DIM] = result[n]


def attend(codes, first, keys, values, pick, bias, sources, cols, bases, out, chunk, heads, kv_head, width):
    slot_len, (row_len, span) = sources[0].shape[1], bias.shape
    chunk_width = heads * HEAD_DIM
    one_head = pl.BlockSpec((None, DOC_MAX + row_len, HEAD_DIM), lambda t, *_: (kv_head, 0, 0))
    operands = [codes, first, keys, values, pick, bias, *sources]
    specs = [one_head, one_head, WHOLE, WHOLE] + [ANYWHERE] * len(sources)
    aliases = {}
    if out is not None:
        aliases = {len(operands): 0}
        operands.append(out)
        specs.append(ANYWHERE)
    return pl.pallas_call(
        functools.partial(attend_kernel, cols=cols, bases=bases, heads=heads),
        grid_spec=pltpu.PrefetchScalarGridSpec(
            num_scalar_prefetch=2,
            grid=(row_len // TILE,),
            in_specs=specs,
            out_specs=pl.BlockSpec((TILE, chunk_width), lambda t, *_: (t, chunk)),
            scratch_shapes=[
                pltpu.VMEM((codes.shape[0], slot_len, chunk_width), jnp.bfloat16),
                pltpu.VMEM((heads * TILE, HEAD_DIM), jnp.bfloat16),
                pltpu.SemaphoreType.DMA,
            ],
        ),
        out_shape=jax.ShapeDtypeStruct((row_len, width), jnp.bfloat16),
        input_output_aliases=aliases,
        compiler_params=pltpu.CompilerParams(vmem_limit_bytes=32 << 20),
        cost_estimate=pl.CostEstimate(
            flops=4 * row_len * span * chunk_width,
            transcendentals=row_len * span * heads,
            bytes_accessed=6 * row_len * chunk_width,
        ),
        name="attend",
    )(*operands)


def lists_of(masks, codes, slots):
    items = masks.shape[1]
    upto = jnp.arange(items)[:, None] <= jnp.arange(items)[None, :]
    rank = jnp.dot(
        masks.astype(jnp.bfloat16), upto.astype(jnp.bfloat16), preferred_element_type=jnp.float32
    ).astype(jnp.int32) - 1
    rank = jnp.where(masks, rank, -1)
    if codes is None:
        return rank
    at = rank[:, None, :] == jnp.arange(slots, dtype=jnp.int32)[None, :, None]
    return jnp.sum(jnp.where(at, codes, 0), axis=2)


def swap(rows, bit):
    pairs = [(i, i ^ bit) for i in range(lax.axis_size("dp"))]
    return lax.ppermute(rows, "dp", pairs)


MESH = pl.DeviceIdType.MESH


def meet_kernel(mine_ref, queries_ref, keys_ref, values_ref, table_ref, load_ref, count_ref, near_ref, *rest):
    kv_ref, send_sem, recv_sem = rest
    me, level = lax.axis_index("dp"), lax.axis_index("tensor")
    core = me & 1
    groups = table_ref.shape[0]
    half = queries_ref.shape[2] // 2
    barrier = pltpu.get_barrier_semaphore()
    for n in range(1, groups):
        pl.semaphore_signal(barrier, inc=1, device_id=(me ^ n, level), device_id_type=MESH)
    pl.semaphore_wait(barrier, groups - 1)
    copies = []
    for n in range(1, groups):
        copies.append(
            pltpu.make_async_remote_copy(
                mine_ref, table_ref.at[me], send_sem.at[n], recv_sem.at[n],
                device_id=(me ^ n, level), device_id_type=MESH,
            )
        )
    base = pl.multiple_of((core ^ 1) * half, HEAD_DIM)
    copies.append(
        pltpu.make_async_remote_copy(
            queries_ref.at[:, :, pl.ds(base, near_ref.shape[2])], near_ref, send_sem.at[0], recv_sem.at[0],
            device_id=(me ^ 1, level), device_id_type=MESH,
        )
    )
    for copy in copies:
        copy.start()
    table_ref[me] = mine_ref[...]
    for n in range(kv_ref.shape[0]):
        for part in range(2):
            head = pl.multiple_of((2 * n + (core ^ part)) * HEAD_DIM, HEAD_DIM)
            for kind, rows in enumerate((keys_ref, values_ref)):
                kv_ref[n, part, :, :, kind * HEAD_DIM : (kind + 1) * HEAD_DIM] = rows[:, :, pl.ds(head, HEAD_DIM)]
    for copy in copies[:-1]:
        copy.wait()
    dest, tokens = table_ref[:, 0, :], table_ref[:, 1, :]
    lane = lax.broadcasted_iota(jnp.int32, load_ref.shape, 1)
    load, count = jnp.zeros(load_ref.shape, jnp.int32), jnp.zeros(load_ref.shape, jnp.int32)
    for g in range(groups):
        load = jnp.where(lane == g, jnp.sum(jnp.where(dest == g, tokens, 0), axis=1, keepdims=True), load)
        count = jnp.where(lane == g, jnp.sum((dest == g).astype(jnp.int32), axis=1, keepdims=True), count)
    load_ref[...] = load
    count_ref[...] = count
    copies[-1].wait()


def meet(mine, queries, key_rows, value_rows, groups, ways, width):
    sentences, slot_len, _ = queries.shape
    bf16, i32 = jnp.bfloat16, jnp.int32
    small = jax.ShapeDtypeStruct((groups, groups), i32)
    kv = jax.ShapeDtypeStruct((ways, 2, key_rows.shape[0], slot_len, 2 * HEAD_DIM), bf16)
    return pl.pallas_call(
        meet_kernel,
        in_specs=[WHOLE, ANYWHERE, WHOLE, WHOLE],
        out_specs=[WHOLE, WHOLE, WHOLE, ANYWHERE, WHOLE],
        out_shape=[
            jax.ShapeDtypeStruct((groups, 2, sentences), i32), small, small,
            jax.ShapeDtypeStruct((sentences, slot_len, width), bf16),
            kv,
        ],
        scratch_shapes=[
            pltpu.SemaphoreType.DMA((groups,)),
            pltpu.SemaphoreType.DMA((groups,)),
        ],
        compiler_params=pltpu.CompilerParams(collective_id=0, has_side_effects=True),
        name="meet",
    )(mine, queries, key_rows, value_rows)


def plan_kernel(table_ref, load_ref, count_ref, plan_ref, tier_ref, slot_ref, begin_ref, shift_ref, key_ref, *, tiers):
    me = lax.axis_index("dp")
    chip, core = me >> 1, me & 1
    groups, _, sentences = table_ref.shape
    chips = groups // 2
    load = [[load_ref[2 * a, g] + load_ref[2 * a + 1, g] for g in range(groups)] for a in range(chips)]
    begin, totals = [[None] * groups for _ in range(chips)], [None] * groups
    for g in range(groups):
        total = jnp.int32(0)
        for a in range(chips):
            begin[a][g] = total
            total = total + load[a][g]
        totals[g] = total
    need = [jnp.int32(0)] * chips
    for a in range(chips):
        for b in range(chips):
            one = begin[a][2 * b] & (LEAST - 1)
            end = one + load[a][2 * b]
            two = end + ((begin[a][2 * b + 1] - end) & (LEAST - 1))
            need[a ^ b] = jnp.maximum(need[a ^ b], two + load[a][2 * b + 1])
            for g, first in ((2 * b, one), (2 * b + 1, two)):
                shift_ref[a * groups + g] = first
                begin_ref[a * groups + g] = begin[a][g]
    tier = jnp.int32(len(tiers) - 1)
    for n in reversed(range(len(tiers) - 1)):
        fits = functools.reduce(jnp.logical_and, [low <= cap for low, cap in zip(need, tiers[n])])
        tier = jnp.where(fits, n, tier)
    tier_ref[0] = tier
    passed = jnp.int32(0)
    for key in range(groups):
        group = key ^ (2 * chip)
        key_ref[key] = passed
        key_ref[groups + key] = shift_ref[chip * groups + group]
        for n in range(1, 16) if key % 2 else range(1):
            plan_ref[FIRST + 16 * (key // 2) + n] = passed
        passed = passed + count_ref[2 * chip, group] + count_ref[2 * chip + 1, group]
    for half in range(2):
        mine = sentences * (half ^ core)

        def place(n, carry, half=half, mine=mine):
            key = table_ref[2 * chip + half, 0, n] ^ (2 * chip)
            size = table_ref[2 * chip + half, 1, n]
            flow = key >> 1
            at, row = key_ref[key], key_ref[groups + key]
            plan_ref[CODE + at] = mine + n
            plan_ref[START + at] = flow * FAR + row
            plan_ref[COUNT + at] = size
            key_ref[key] = at + 1
            key_ref[groups + key] = row + size
            tile = ((row + SEND_TILE - 1) * 37450) >> 22
            plan_ref[FIRST + 16 * flow + jnp.where(tile * SEND_TILE < row + size, tile, 15)] = at
            return carry

        lax.fori_loop(0, sentences, place, 0, unroll=8)
    for order in range(2):
        group = 2 * chip + (core if order == 1 else 1 - core)
        for flow in range(chips):
            at = chip ^ flow
            plan_ref[INTO + 16 * order + flow] = begin_ref[at * groups + group]
            plan_ref[INTO + 16 * order + 4 + flow] = load_ref[2 * at, group] + load_ref[2 * at + 1, group]
            plan_ref[INTO + 16 * order + 8 + flow] = shift_ref[at * groups + group]
        plan_ref[INTO + 16 * order + 12] = begin_ref[(chips - 1) * groups + group] + (
            load_ref[2 * chips - 2, group] + load_ref[2 * chips - 1, group]
        )
    lane = lax.broadcasted_iota(jnp.int32, (1, HEAD_DIM), 1)
    token = lane % SLOT
    for r in range(slot_ref.shape[0]):
        start, size = jnp.zeros((1, HEAD_DIM), jnp.int32), jnp.zeros((1, HEAD_DIM), jnp.int32)
        for n in range(HEAD_DIM // SLOT):
            at = r * (HEAD_DIM // SLOT) + n
            start = jnp.where(lane // SLOT == n, plan_ref[START + at], start)
            size = jnp.where(lane // SLOT == n, plan_ref[COUNT + at], size)
        slot_ref[r : r + 1, :] = jnp.where(token < size, start + token, -1)


def make_plan(table, load, count, tiers):
    groups, _, sentences = table.shape
    cells = groups // 2 * groups
    return pl.pallas_call(
        functools.partial(plan_kernel, tiers=tiers),
        in_specs=[SCALARS] * 3,
        out_specs=[SCALARS, SCALARS, WHOLE],
        out_shape=[
            jax.ShapeDtypeStruct((PLAN,), jnp.int32),
            jax.ShapeDtypeStruct((1,), jnp.int32),
            jax.ShapeDtypeStruct((2 * sentences * SLOT // HEAD_DIM, HEAD_DIM), jnp.int32),
        ],
        scratch_shapes=[pltpu.SMEM((cells,), jnp.int32)] * 2 + [pltpu.SMEM((2 * groups,), jnp.int32)],
        name="plan",
    )(table, load, count)


def post_kernel(plan_ref, slot_ref, *rest, caps, fetch_one):
    sources, rest = rest[: -2 * len(caps) - 3], rest[-2 * len(caps) - 3 :]
    outs, (*tiles, buf, sem, out_sem) = rest[: len(caps)], rest[len(caps) :]
    slot_len, width = buf.shape[1:]

    def one(n, carry):
        fetch_one(plan_ref[CODE + n], sources, buf.at[n], sem)
        return carry

    lax.fori_loop(0, buf.shape[0], one, 0, unroll=4)
    pltpu.make_async_copy(buf, buf, sem).wait()
    per = HEAD_DIM // slot_len
    deep = SPREAD // per
    for flow, (cap, out) in enumerate(zip(caps, tiles)):

        def fill(tile, low, size, flow=flow, out=out):
            row = lax.broadcasted_iota(jnp.int32, (size, HEAD_DIM), 0) + (flow * FAR + low)
            first = jnp.minimum(plan_ref[FIRST + 16 * flow + tile] // per, slot_ref.shape[0] - deep)
            pick = jnp.concatenate(
                [
                    (row == slot_ref[pl.ds(first + n, 1), :]).astype(jnp.float32).astype(jnp.bfloat16)
                    for n in range(deep)
                ],
                axis=1,
            )
            rows = buf[pl.ds(first * per, SPREAD)].reshape(SPREAD * slot_len, width)
            out[pl.ds(low, size), :] = jnp.dot(pick, rows, preferred_element_type=jnp.float32).astype(
                jnp.bfloat16
            )

        whole = cap // SEND_TILE
        if whole <= UNROLLED:
            for tile in range(whole):
                fill(tile, tile * SEND_TILE, SEND_TILE)
        else:

            @pl.loop(0, whole)
            def _(tile, fill=fill):
                fill(tile, pl.multiple_of(tile * SEND_TILE, LEAST), SEND_TILE)

        left = cap % SEND_TILE
        if left:
            fill(whole, cap - left, left)
        pltpu.make_async_copy(out, outs[flow], out_sem.at[flow]).start()
    for flow, out in enumerate(tiles):
        pltpu.make_async_copy(out, outs[flow], out_sem.at[flow]).wait()


def post(plan, slots, sources, fetch_one, caps, count, slot_len, width):
    shapes = [jax.ShapeDtypeStruct((cap, width), jnp.bfloat16) for cap in caps]
    return pl.pallas_call(
        functools.partial(post_kernel, caps=caps, fetch_one=fetch_one),
        grid_spec=pltpu.PrefetchScalarGridSpec(
            num_scalar_prefetch=1,
            grid=(1,),
            in_specs=[WHOLE] + [FAR_OFF] * len(sources),
            out_specs=[FAR_OFF] * len(caps),
            scratch_shapes=[pltpu.VMEM(shape.shape, shape.dtype) for shape in shapes] + [
                pltpu.VMEM((count, slot_len, width), jnp.bfloat16),
                pltpu.SemaphoreType.DMA,
                pltpu.SemaphoreType.DMA((len(caps),)),
            ],
        ),
        out_shape=shapes,
        compiler_params=pltpu.CompilerParams(vmem_limit_bytes=VMEM),
        cost_estimate=pl.CostEstimate(
            flops=0,
            transcendentals=0,
            bytes_accessed=SMALL,
        ),
        name="post",
    )(plan, slots, *sources)


def lend_kernel(rows_ref, out_ref, send_sem, recv_sem, *, region):
    me, level = lax.axis_index("dp"), lax.axis_index("tensor")
    barrier = pltpu.get_barrier_semaphore()
    pl.semaphore_signal(barrier, inc=1, device_id=(me ^ 1, level), device_id_type=MESH)
    pl.semaphore_wait(barrier, 1)
    copy = pltpu.make_async_remote_copy(
        rows_ref.at[region((me & 1) ^ 1)] if region else rows_ref, out_ref, send_sem, recv_sem,
        device_id=(me ^ 1, level), device_id_type=MESH,
    )
    copy.start()
    copy.wait()


def lend(rows, shape, region, number):
    return pl.pallas_call(
        functools.partial(lend_kernel, region=region),
        in_specs=[ANYWHERE],
        out_specs=ANYWHERE,
        out_shape=jax.ShapeDtypeStruct(shape, rows.dtype),
        scratch_shapes=[pltpu.SemaphoreType.DMA] * 2,
        compiler_params=pltpu.CompilerParams(
            collective_id=number, has_side_effects=True, vmem_limit_bytes=4 << 20
        ),
        cost_estimate=pl.CostEstimate(flops=0, transcendentals=0, bytes_accessed=SMALL),
        name="lend",
    )(rows)


def sort_kernel(plan_ref, *rest, caps, lead):
    flows, (away, own_ref, buf, sem) = rest[: len(caps)], rest[len(caps) :]
    row_len, width = own_ref.shape[0] - lead, own_ref.shape[1]
    for f, (cap, flow) in enumerate(zip(caps, flows)):
        pltpu.make_async_copy(flow, buf.at[f, pl.ds(TILE, cap)], sem.at[f]).start()
    for f, cap in enumerate(caps):
        for low in (0, TILE + cap):
            buf[f, low : low + TILE, :] = jnp.zeros((TILE, width), jnp.bfloat16)
    if lead:
        for out in (away, own_ref):
            out[:lead, :] = jnp.zeros((lead, width), jnp.bfloat16)
    for f, (cap, flow) in enumerate(zip(caps, flows)):
        pltpu.make_async_copy(flow, buf.at[f, pl.ds(TILE, cap)], sem.at[f]).wait()
    row = lax.broadcasted_iota(jnp.int32, (TILE, HEAD_DIM), 0)

    def fill(order, out):
        @pl.loop(0, row_len // TILE)
        def _(t):
            here = pl.multiple_of(t * TILE, TILE)
            total = None
            for f, cap in enumerate(caps):
                begin = plan_ref[INTO + 16 * order + f] - here
                size = plan_ref[INTO + 16 * order + 4 + f]
                low = plan_ref[INTO + 16 * order + 8 + f] - begin + TILE
                low = pl.multiple_of(jnp.clip(low, 0, TILE + cap), LEAST)
                mask = ((row >= begin) & (row < begin + size)).astype(jnp.float32).astype(jnp.bfloat16)
                mask = jnp.concatenate([mask] * (width // HEAD_DIM), axis=1)
                part = buf[f, pl.ds(low, TILE), :] * mask
                total = part if total is None else total + part
            out[pl.ds(lead + here, TILE), :] = total

    fill(0, away)
    fill(1, own_ref)


def sort(plan, flows, row_len, lead):
    caps = tuple(flow.shape[0] for flow in flows)
    width = flows[0].shape[1]
    shape = jax.ShapeDtypeStruct((lead + row_len, width), jnp.bfloat16)
    return pl.pallas_call(
        functools.partial(sort_kernel, caps=caps, lead=lead),
        in_specs=[SCALARS] + [ANYWHERE] * len(flows),
        out_specs=[WHOLE, WHOLE],
        out_shape=[shape, shape],
        scratch_shapes=[
            pltpu.VMEM((len(caps), max(caps) + 2 * TILE, width), jnp.bfloat16),
            pltpu.SemaphoreType.DMA((len(caps),)),
        ],
        compiler_params=pltpu.CompilerParams(
            vmem_limit_bytes=VMEM if width > 1024 else 24 << 20,
        ),
        cost_estimate=pl.CostEstimate(flops=0, transcendentals=0, bytes_accessed=SMALL),
        name="sort",
    )(plan, *flows)


def mix_kernel(plan_ref, bias_ref, *rest, cols, half):
    pairs, (*_, out_ref, buf, sem) = rest[:4], rest[4:]
    tile, last = pl.program_id(0), pl.num_programs(0) - 1
    span = bias_ref.shape[1]
    width = pairs[0].shape[1]
    step_rows = buf.shape[2]
    bias = [bias_ref[low : low + TILE, :] for low in range(0, step_rows, TILE)]
    live = [jnp.max(one, axis=1, keepdims=True) > -1.0 for one in bias]
    scale = (HEAD_DIM**-0.5) * LOG2E
    stack = min(STACK, width // HEAD_DIM)
    core = lax.axis_index("dp") & 1
    turn = tile & 1

    def send(step, side, way):
        col = pl.multiple_of((core ^ side) * half + cols, HEAD_DIM)
        row = pl.multiple_of(step * step_rows, TILE)
        copy = pltpu.make_async_copy(
            buf.at[step & 1, side], out_ref.at[pl.ds(row, step_rows), pl.ds(col, width)], sem.at[step & 1, side]
        )
        copy.start() if way else copy.wait()

    @pl.when(tile >= 2)
    def _():
        for side in range(2):
            send(tile - 2, side, False)

    groups = []
    for part in range(step_rows // TILE):
        for side in range(2):
            for g in range(width // HEAD_DIM // stack):
                groups.append((part, side, g, *pairs[2 * side : 2 * side + 2]))

    def keys_of(part):
        return pl.ds(pl.multiple_of(tile * step_rows + part * TILE, TILE), span)

    def score_of(group):
        part, side, g, q_ref, kv_ref = group
        rows = jnp.concatenate(
            [
                q_ref[part * TILE : (part + 1) * TILE, h * HEAD_DIM : (h + 1) * HEAD_DIM]
                for h in range(g * stack, (g + 1) * stack)
            ],
            axis=0,
        )
        return lax.dot_general(
            rows, kv_ref[keys_of(part), :HEAD_DIM], (((1,), (1,)), ((), ())),
            preferred_element_type=jnp.float32,
        ).reshape(stack, TILE, span)

    def finish(group, weight, norm):
        part, side, g, q_ref, kv_ref = group
        mixed = jnp.dot(
            weight, kv_ref[keys_of(part), HEAD_DIM:], preferred_element_type=jnp.float32
        ).reshape(stack, TILE, HEAD_DIM)
        result = jnp.where(live[part][None], mixed / norm, 0.0).astype(jnp.bfloat16)
        for n in range(stack):
            h = g * stack + n
            buf[turn, side, part * TILE : (part + 1) * TILE, h * HEAD_DIM : (h + 1) * HEAD_DIM] = result[n]

    following, held = score_of(groups[0]), None
    for n, group in enumerate(groups):
        score = following
        following = score_of(groups[n + 1]) if n + 1 < len(groups) else None
        score = score * scale + bias[group[0]][None]
        peak = jnp.max(score, axis=2, keepdims=True)
        weight = jnp.exp2(score - peak)
        norm = jnp.sum(weight, axis=2, keepdims=True)
        if held is not None:
            finish(*held)
        held = group, weight.astype(jnp.bfloat16).reshape(stack * TILE, span), norm
    finish(*held)
    for side in range(2):
        send(tile, side, True)

    @pl.when(tile == last)
    def _():
        for side in range(2):
            send(tile - 1, side, False)
            send(tile, side, False)


def mix(plan, bias, own, far, out, full_width, col):
    (row_len, width), span = own[0].shape, bias.shape[1]
    operands = [plan, bias, *own, *far]
    step_rows = 2 * TILE if width <= 1024 else TILE
    rows = pl.BlockSpec((step_rows, width), lambda t, *_: (t, 0))
    whole = pl.BlockSpec(own[1].shape, lambda t, *_: (0, 0))
    specs = [pl.BlockSpec((step_rows, span), lambda t, *_: (t, 0)), rows, whole, rows, whole]
    aliases = {}
    if out is not None:
        aliases = {len(operands): 0}
        operands.append(out)
        specs.append(ANYWHERE)
    return pl.pallas_call(
        functools.partial(mix_kernel, cols=col, half=full_width // 2),
        grid_spec=pltpu.PrefetchScalarGridSpec(
            num_scalar_prefetch=1,
            grid=(row_len // step_rows,),
            in_specs=specs,
            out_specs=ANYWHERE,
            scratch_shapes=[
                pltpu.VMEM((2, 2, step_rows, width), jnp.bfloat16),
                pltpu.SemaphoreType.DMA((2, 2)),
            ],
        ),
        out_shape=jax.ShapeDtypeStruct((row_len, full_width), jnp.bfloat16),
        input_output_aliases=aliases,
        compiler_params=pltpu.CompilerParams(vmem_limit_bytes=32 << 20),
        cost_estimate=pl.CostEstimate(flops=0, transcendentals=0, bytes_accessed=SMALL),
        name="mix",
    )(*operands)


def after(value, *others):
    return lax.optimization_barrier((value, *others))[1:]


def eight_groups(queries, key_rows, value_rows, destination, token_count, doc_ids):
    ways = lax.axis_size("tensor")
    core = lax.axis_index("dp") & 1
    sentences, slot_len, q_width = queries.shape
    lanes = key_rows.shape[0]
    row_len = doc_ids.shape[1]
    half = q_width // 2
    kv_width = key_rows.shape[2] // ways
    full = 4 * (sentences // 4) * slot_len
    tiers = [(TIERS[-1], cap, cap, cap) for cap in TIERS] + [(full + 32,) * 4]
    def fetch_q(code, sources, into, sem, col, skip):
        own, near = sources
        width = into.shape[1]

        @pl.when(code < sentences)
        def _():
            base = pl.multiple_of((lax.axis_index("dp") & 1) * half + col, HEAD_DIM)
            pltpu.make_async_copy(own.at[code, :, pl.ds(base, width)], into, sem).start()

        @pl.when(code >= sentences)
        def _():
            pltpu.make_async_copy(
                near.at[code - sentences, :, pl.ds(col - skip, width)], into, sem
            ).start()

    def fetch_kv(code, sources, into, sem):
        own, near = sources
        from_level = (code & (sentences - 1)) // lanes
        lane = code & (lanes - 1)

        @pl.when(code < sentences)
        def _():
            pltpu.make_async_copy(own.at[from_level, 0, lane], into, sem).start()

        @pl.when(code >= sentences)
        def _():
            pltpu.make_async_copy(near.at[from_level, lane], into, sem).start()

    mine = jnp.stack([destination, token_count])
    table, load, number, near_first, kv = meet(
        mine, queries, key_rows, value_rows, lax.axis_size("dp"), ways, ROUNDS[0]
    )
    plan, tier, slots = make_plan(table, load, number, tiers)

    def with_caps(caps, widths, queries, near_first, plan, slots, doc_ids, kv):
        cols = [sum(widths[:n]) for n in range(len(widths))]
        rounds = len(widths)
        sent, arrived = [None] * rounds, [None] * rounds
        fresh = widths[0] != near_first.shape[2]
        skip = 0 if fresh else widths[0]

        def rest_of(core):
            start = pl.multiple_of(core * half + skip, HEAD_DIM)
            return slice(None), slice(None), pl.ds(start, half - skip)

        def others(core):
            return slice(None), 1

        def lend_rest(order, rows):
            return lend(
                rows, (sentences, slot_len, half - skip), rest_of, 4 if fresh else 1
            )

        def load(n, order):
            ready, base = (near_first, 0) if n == 0 and not fresh else (near, skip)
            sent[n] = post(
                order, slots, [queries, ready], functools.partial(fetch_q, col=cols[n], skip=base), caps,
                2 * sentences, slot_len, widths[n],
            )
            return after(sent[n][0], plan)[0]

        def depart(flows):
            far, beside, across = (swap(flows[f], 2 * f) for f in (3, 1, 2))
            return [flows[0], beside, across, far]

        if fresh:
            near = lend_rest(plan, queries)
        order = load(0, plan)
        arrived[0] = depart(sent[0])
        if rounds > 1:
            kept, order, kv, rows = lax.optimization_barrier((sent[0][0], plan, kv, queries))
            arrived[0][0] = kept
            near = lend_rest(order, rows)
        kv = lax.all_to_all(kv, "tensor", split_axis=0, concat_axis=0, tiled=True)
        if rounds > 1:
            order = load(1, order)
            order, *flows = after(arrived[0], order, *sent[1])
            arrived[1] = depart(flows)
        for n in range(2, min(rounds, 3)):
            order = load(n, order)
        waiting = list(range(3, rounds))
        docs, = after(order, doc_ids[0])

        live = jnp.arange(row_len, dtype=jnp.int32) < plan[INTO + 16 + 12]
        span = DOC_MAX + TILE
        padded = jnp.concatenate([jnp.full((DOC_MAX,), -1, jnp.int32), docs])
        tiles = row_len // TILE
        key_docs = jnp.stack([padded[t * TILE : t * TILE + span] for t in range(tiles)])
        col = jnp.arange(span, dtype=jnp.int32)[None, None, :]
        row = jnp.arange(TILE, dtype=jnp.int32)[None, :, None]
        allowed = (
            (col - DOC_MAX <= row)
            & (key_docs[:, None, :] == docs.reshape(tiles, TILE)[:, :, None])
            & live.reshape(tiles, TILE)[:, :, None]
        )
        bias = jnp.where(allowed, 0.0, NEG).astype(jnp.float32).reshape(row_len, span)

        order, = after(bias, order)
        steps = list(range(rounds))
        kv_turn = min(2, rounds)
        steps.insert(kv_turn, None)
        out, mixed = None, 0
        q_rows, kv_rows, kv_arrived = [None] * rounds, None, None

        def settle(step, order):
            nonlocal kv_rows
            if step is None:
                kv_away, kv_own = sort(order, kv_arrived, row_len, DOC_MAX)
                kv_rows = kv_own, lend(kv_away, kv_away.shape, None, 5)
                return after(kv_rows[1], plan)[0]
            q_away, q_own = sort(order, arrived[step], row_len, 0)
            q_far = lend(q_away, q_away.shape, None, 5 + sorted({*ROUNDS, half}).index(widths[step]) + 1)
            q_rows[step] = q_own, q_far
            return after(q_far, plan)[0]

        def load_kv(order):
            near_kv = lend(after(order, kv)[0], kv.shape[:1] + kv.shape[2:], others, 2)
            flows = post(
                order, slots, [kv, near_kv], fetch_kv, caps, 2 * sentences, slot_len, 2 * HEAD_DIM
            )
            return flows, after(flows[0], plan)[0]

        kv_sent = None
        for at in range(len(steps)):
            if at + 1 < len(steps):
                step = steps[at + 1]
                if step is None:
                    if kv_sent is None:
                        kv_sent, order = load_kv(order)
                    flows = kv_sent
                else:
                    flows = sent[step]
                here = kv_arrived if steps[at] is None else arrived[steps[at]]
                if step is None or arrived[step] is None:
                    order, *flows = after(here, order, *flows)
                    flows = depart(flows)
                    if step is None:
                        kv_arrived = flows
                    else:
                        arrived[step] = flows
            order = settle(steps[at], order)
            while kv_rows is not None and mixed < rounds and q_rows[mixed] is not None:
                q_own, q_far = q_rows[mixed]
                out = mix(
                    order, bias, (q_own, kv_rows[0]), (q_far, kv_rows[1]), out, q_width, cols[mixed]
                )
                order, = after(out, plan)
                mixed += 1
            if at and waiting:
                order = load(waiting.pop(0), order)
        return out

    return lax.switch(
        tier[0],
        [functools.partial(with_caps, caps, ROUNDS) for caps in tiers[:-1]]
        + [functools.partial(with_caps, tiers[-1], (half,))],
        queries, near_first, plan, slots, doc_ids, kv,
    )


def per_device(queries, key_rows, value_rows, destination, token_count, doc_ids):
    groups = lax.axis_size("dp")
    ways = lax.axis_size("tensor")
    me = lax.axis_index("dp")
    sentences = destination.shape[0]
    slot_len = queries.shape[1]
    row_len = doc_ids.shape[1]
    q_width = queries.shape[2]
    kv_width = key_rows.shape[2] // ways
    kv_local = kv_width // HEAD_DIM
    per_group = q_width // kv_width
    heads = min(CHUNK_HEADS, per_group)
    chunk_width = heads * HEAD_DIM

    if groups == 8:
        return eight_groups(queries, key_rows, value_rows, destination, token_count, doc_ids)

    table = lax.all_gather(jnp.stack([destination, token_count]), "dp", axis=0)

    def split(rows):
        return rows.reshape(rows.shape[0], slot_len, ways, kv_width)

    def own_heads(key_rows, value_rows):
        kv = jnp.concatenate([split(key_rows), split(value_rows)], axis=3)
        return lax.all_to_all(
            jnp.transpose(kv, (2, 0, 1, 3)), "tensor", split_axis=0, concat_axis=0, tiled=True
        ).reshape(sentences, slot_len, 2 * kv_width)

    dest = table[:, 0, :].reshape(-1)
    counts = table[:, 1, :].reshape(-1)
    source = jnp.repeat(jnp.arange(groups, dtype=jnp.int32), sentences)
    lane = jnp.tile(jnp.arange(sentences, dtype=jnp.int32), groups)

    count_of = lists_of((dest == me)[None], counts[None, None, :], sentences)[0]
    nth = jnp.arange(sentences, dtype=jnp.int32)
    ends = jnp.sum(jnp.where(nth[None, :] <= nth[:, None], count_of[None, :], 0), axis=1)
    place = jnp.arange(row_len, dtype=jnp.int32)
    passed = place[:, None] >= ends[None, :]
    which = jnp.sum(passed.astype(jnp.int32), axis=1)
    start = jnp.sum(jnp.where(passed, count_of[None, :], 0), axis=1)
    live = which < sentences
    spread = min(sentences, (TILE - 1 + LEAST - 1) // LEAST + 1)
    heads_of = place[::TILE]
    first = jnp.sum((heads_of[:, None] >= ends[None, :]).astype(jnp.int32), axis=1)
    first = jnp.minimum(first, sentences - spread)
    window = spread * slot_len
    relative = (which - jnp.repeat(first, TILE)) * slot_len + place - start
    pick = (
        live[:, None] & (relative[:, None] == jnp.arange(window, dtype=jnp.int32)[None, :])
    ).astype(jnp.bfloat16)
    span = DOC_MAX + TILE
    padded = jnp.concatenate([jnp.full((DOC_MAX,), -1, jnp.int32), doc_ids[0]])
    tiles = row_len // TILE
    key_docs = jnp.stack([padded[t * TILE : t * TILE + span] for t in range(tiles)])
    col = jnp.arange(span, dtype=jnp.int32)[None, None, :]
    row = jnp.arange(TILE, dtype=jnp.int32)[None, :, None]
    allowed = (
        (col - DOC_MAX <= row)
        & (key_docs[:, None, :] == doc_ids[0].reshape(tiles, TILE)[:, :, None])
        & live.reshape(tiles, TILE)[:, :, None]
    )
    bias = jnp.where(allowed, 0.0, NEG).astype(jnp.float32).reshape(row_len, span)

    chunks = q_width // chunk_width

    def attend_one(chunk, kv_packed, first, got, codes, out):
        return attend(
            codes, first, *kv_packed, pick, bias, *got, out, chunk, heads, chunk * heads // per_group, q_width
        )

    capacity = max(2, (2 * sentences + groups - 1) // groups)
    rank = lists_of(destination[None, :] == jnp.arange(groups, dtype=jnp.int32)[:, None], None, None)
    slot = jnp.arange(capacity, dtype=jnp.int32)
    at = rank[:, None, :] == slot[None, :, None]
    picked = jnp.sum(jnp.where(at, nth[None, None, :], 0), axis=2).reshape(-1)
    by_source = (dest == me).reshape(groups, sentences)
    rank_in = lists_of(by_source, None, None).reshape(-1)
    codes = lists_of(
        (dest == me)[None], (source * capacity + rank_in)[None, None, :], sentences
    )[0]

    def exchange(rows, col, width):
        sent = gather(picked, [rows], (col,), (0,), width)
        got = lax.all_to_all(sent, "dp", split_axis=0, concat_axis=0, tiled=True)
        return [got], (0,), (0,)

    got_kv = exchange(own_heads(key_rows, value_rows), 0, 2 * kv_width)
    got_q = [exchange(queries, n * chunk_width, chunk_width) for n in range(chunks)]
    kv_packed = pack(codes, first, pick, *got_kv, kv_local)
    out = None
    for n in range(chunks):
        out = attend_one(n, kv_packed, first, got_q[n], codes, out)
    return out


def solution(mesh):
    placed = (
        P("dp", None, "tensor"),
        P(("dp", "tensor"), None, None),
        P(("dp", "tensor"), None, None),
        P("dp"),
        P("dp"),
        P("dp", None),
    )
    return jax.shard_map(
        per_device, mesh=mesh, in_specs=placed, out_specs=P("dp", "tensor"), check_vma=False
    )
```
